512 devices in a mesh: row: 16 (over y, x), col: 32 (over z, core).
Axes of the slice: x: 4, y: 4, z: 16, core: 2. Of those that a mesh axis runs over, the one named last changes fastest.
Arguments:
- div_blocks: float32 [1024, 6, 128, 128], P(('row', 'col')), may hold values from -0.5 to 0.5
- div_owner: int32 [1024, 6], P(('row', 'col')), may hold values from 0 to 15, as said below
- div_local: int32 [1024, 6], P(('row', 'col')), may hold values from 0 to 1
- div_count: int32 [1024], P(('row', 'col')), may hold values from 2 to 6
- inv_blocks: float32 [1024, 5, 128, 128], P(('row', 'col')), may hold values from -6 to 6
- inv_cols: int32 [1024, 5], P(('row', 'col')), may hold values from 0 to 5, as said below
- inv_count: int32 [1024], P(('row', 'col')), may hold values from 3 to 5
- schur_cols: int32 [1024, 4], P(('row', 'col')), may hold values from 0 to 1023, as said below
- schur_count: int32 [1024], P(('row', 'col')), may hold values from 2 to 4
Outputs:
- schur_blocks: float32 [1024, 4, 128, 128], P(('row', 'col'))
The draws below stay inside these ranges and needn't reach their ends.
Inputs may be any that keep to these rules, and one draw needn't show every extreme that they name: `div_owner`: over all 6 slots of the 2 rows of one device, live or not, at most 2 name the same owner, and exactly 2 do for some owner on every device. `inv_cols`: the columns of one row are distinct. `schur_cols`: slot 0 of row p is p itself, slot 1 another row of the same subdomain, slot 2 a row of the subdomain with the same a and c + 1 mod 32, slot 3 one of the subdomain with c - 1 mod 32.
All inputs are finite; a program needn't handle non-finite values.
Results may differ from the reference program's by a relative error of at most 0.0003.
Values sent between devices are 32-bit elements; how exact they have to be, the bound alone decides.
A program may use at most 128 MiB of HBM per device.

```python
import jax
import jax.numpy as jnp
from jax import lax

BS = 128
PB_DEV = 2
VB_DEV = 2
KB = 6
KM = 5
KS = 4
OWNERS = 16
LONGITUDES = 32
CAP = 2
NP = 1024
NV = 1024


def draw_div_owner(key, part):
    groups = NP // PB_DEV
    listed = PB_DEV * KB
    first_key, second_key = jax.random.split(jax.random.fold_in(key, 11))
    owner_base = jnp.tile(jnp.arange(OWNERS, dtype=jnp.int32)[None, :], (groups, 1))
    owner_order = jax.random.permutation(first_key, owner_base, axis=1, independent=True)
    picks = jnp.arange(listed, dtype=jnp.int32) // CAP
    sequence = owner_order[:, picks]
    spot_base = jnp.tile(jnp.arange(listed, dtype=jnp.int32)[None, :], (groups, 1))
    spot_order = jax.random.permutation(second_key, spot_base, axis=1, independent=True)
    owners_drawn = jnp.take_along_axis(sequence, spot_order, axis=1)
    return owners_drawn.reshape(NP, KB)


def draw_inv_cols(key, part):
    column_base = jnp.tile(jnp.arange(3 * VB_DEV, dtype=jnp.int32)[None, :], (NV, 1))
    column_order = jax.random.permutation(jax.random.fold_in(key, 17), column_base, axis=1, independent=True)
    return column_order[:, :KM]


def draw_schur_cols(key, part):
    first_key, second_key, third_key = jax.random.split(jax.random.fold_in(key, 23), 3)
    row_ids = jnp.arange(NP, dtype=jnp.int32)
    device_ids = row_ids // PB_DEV
    local_ids = row_ids % PB_DEV
    slab_ids = device_ids // LONGITUDES
    lon_ids = device_ids % LONGITUDES
    step_other = jax.random.randint(first_key, (NP,), 1, PB_DEV, dtype=jnp.int32)
    other_row = device_ids * PB_DEV + (local_ids + step_other) % PB_DEV
    right_row = (slab_ids * LONGITUDES + (lon_ids + 1) % LONGITUDES) * PB_DEV + jax.random.randint(second_key, (NP,), 0, PB_DEV, dtype=jnp.int32)
    left_row = (slab_ids * LONGITUDES + (lon_ids + LONGITUDES - 1) % LONGITUDES) * PB_DEV + jax.random.randint(third_key, (NP,), 0, PB_DEV, dtype=jnp.int32)
    return jnp.stack([row_ids, other_row, right_row, left_row], axis=1)


def plant(result, rng, least, largest):
    longest = result.shape.index(max(result.shape))
    spots = []
    for shift in (0, 1):
        where = [jax.random.randint(jax.random.fold_in(rng, axis), (), 0, length) for axis, length in enumerate(result.shape)]
        where[longest] = (where[longest] + shift) % result.shape[longest]
        spots.append(tuple(where))
    return result.at[spots[0]].set(least).at[spots[1]].set(largest)


def level_of(rng, shape, cuts, least, top_value):
    def one(axis_at, shards_of):
        heights = jax.random.uniform(jax.random.fold_in(jax.random.fold_in(rng, 6), axis_at), (shards_of,), jnp.float32, least / len(cuts), top_value / len(cuts))
        return jnp.repeat(jnp.exp(heights), shape[axis_at] // shards_of).reshape((-1,) + (1,) * (len(shape) - axis_at - 1))

    gain = one(*cuts[0])
    for cut in cuts[1:]:
        gain = gain * one(*cut)
    return gain


def noise(key, shape, deviation, most, shards=(), kind=jnp.bfloat16):
    level = level_of(key, shape, shards, -0.22, 0.18) if shards else 1.0
    drawn = jax.random.normal(key, shape, jnp.float32) * deviation * level
    return jnp.minimum(jnp.maximum(drawn, -most), most).astype(kind)


def setup_inputs(seed: int = 0) -> dict:
    splits = jax.random.split(jax.random.key(seed), 10)
    return {
        "div_blocks": noise(splits[0], (NP, KB, BS, BS), BS ** -0.5, 0.5, ((0, 512),), jnp.float32),
        "div_owner": draw_div_owner(jax.random.fold_in(splits[9], 71), 0),
        "div_local": plant(jax.random.randint(splits[2], (NP, KB), 0, VB_DEV), jax.random.fold_in(splits[2], 1), 0, VB_DEV - 1).astype(jnp.int32),
        "div_count": plant(jax.random.randint(splits[3], (NP,), 2, KB + 1), jax.random.fold_in(splits[3], 1), 2, KB).astype(jnp.int32),
        "inv_blocks": noise(splits[4], (NV, KM, BS, BS), 1.0, 6.0, ((0, 512),), jnp.float32),
        "inv_cols": draw_inv_cols(jax.random.fold_in(splits[9], 71), 0),
        "inv_count": plant(jax.random.randint(splits[6], (NV,), 3, KM + 1), jax.random.fold_in(splits[6], 1), 3, KM).astype(jnp.int32),
        "schur_cols": draw_schur_cols(jax.random.fold_in(splits[9], 71), 0),
        "schur_count": plant(jax.random.randint(splits[8], (NP,), 2, KS + 1), jax.random.fold_in(splits[8], 1), 2, KS).astype(jnp.int32),
    }


def reference(div_blocks, div_owner, div_local, div_count, inv_blocks, inv_cols, inv_count, schur_cols, schur_count):
    press_ids = jnp.arange(NP, dtype=jnp.int32)
    lon_index = (press_ids // PB_DEV) % LONGITUDES
    vel_ids = (div_owner * LONGITUDES + lon_index[:, None]) * VB_DEV + div_local
    slot_live = jnp.arange(KB, dtype=jnp.int32)[None, :] < div_count[:, None]
    vel_rows = jnp.arange(NV, dtype=jnp.int32)
    vel_dev = vel_rows // VB_DEV
    slab_index = vel_dev // LONGITUDES
    vel_lon = vel_dev % LONGITUDES
    shifted = (vel_lon[:, None] + inv_cols // VB_DEV - 1 + LONGITUDES) % LONGITUDES
    inv_ids = (slab_index[:, None] * LONGITUDES + shifted) * VB_DEV + inv_cols % VB_DEV
    inv_live = jnp.arange(KM, dtype=jnp.int32)[None, :] < inv_count[:, None]
    pattern_live = jnp.arange(KS, dtype=jnp.int32)[None, :] < schur_count[:, None]

    def one_row(row):
        row_blocks = div_blocks[row]
        vel_here = vel_ids[row]
        live_here = slot_live[row]
        inv_rows = inv_blocks[vel_here]
        inv_here = inv_ids[vel_here]
        inv_ok = inv_live[vel_here] & live_here[:, None]
        partial_value = jnp.einsum("kpq,kmqr->kmpr", row_blocks, inv_rows, precision=lax.Precision.HIGHEST)
        others = schur_cols[row]
        other_ids = vel_ids[others]
        other_live = slot_live[others] & pattern_live[row][:, None]
        matches = (inv_here[None, :, :, None] == other_ids[:, None, None, :]) & inv_ok[None, :, :, None] & other_live[:, None, None, :]
        summed = jnp.einsum("tkml,kmpr->tlpr", matches.astype(jnp.float32), partial_value, precision=lax.Precision.HIGHEST)
        return jnp.einsum("tlpr,tlsr->tps", summed, div_blocks[others], precision=lax.Precision.HIGHEST)

    return lax.map(one_row, press_ids)
```

```python
import functools

import jax
import jax.numpy as jnp
from jax import lax
from jax.experimental import pallas as pl
from jax.experimental.pallas import tpu as pltpu
from jax.sharding import PartitionSpec as P

MESH = pl.DeviceIdType.MESH
F32 = jnp.float32
BF16 = jnp.bfloat16
SIDE = 4


def halves(value):
    high = value.astype(BF16)
    return high, (value - high.astype(F32)).astype(BF16)


def kernel(
    lon_count,
    owner_ref,
    local_ref,
    count_ref,
    cols_ref,
    inv_count_ref,
    pattern_ref,
    pattern_count_ref,
    div_ref,
    inv_ref,
    out_ref,
    inv_all,
    div_all,
    right_parts,
    left_parts,
    factors,
    packet,
    meta,
    places,
    local_sem,
    div_send,
    div_recv,
    meta_send,
    meta_recv,
    inv_send,
    inv_recv,
):
    owners = SIDE * SIDE
    rows, slots_row = owner_ref.shape
    vel_rows, inv_slots = cols_ref.shape
    pattern = pattern_ref.shape[1]
    listed = rows * slots_row
    side = out_ref.shape[2]
    row = lax.axis_index("row")
    col = lax.axis_index("col")
    grid_y, grid_x = row // SIDE, row % SIDE
    nxt = (col + 1) % lon_count
    prv = (col + lon_count - 1) % lon_count

    def at(dy, dx):
        return ((grid_y + dy + SIDE) % SIDE) * SIDE + (grid_x + dx + SIDE) % SIDE

    barrier = pltpu.get_barrier_semaphore()

    def greet(step, carry):
        pl.semaphore_signal(
            barrier, inc=1, device_id=((row + step) % owners, col), device_id_type=MESH
        )
        return carry

    lax.fori_loop(1, owners, greet, 0)
    for other in (nxt, prv):
        pl.semaphore_signal(barrier, inc=1, device_id=(row, other), device_id_type=MESH)

    own_inv = pltpu.make_async_copy(
        inv_ref,
        inv_all.at[pl.ds(row * (vel_rows * inv_slots), vel_rows * inv_slots)],
        local_sem.at[0],
    )
    own_div = pltpu.make_async_copy(div_ref, div_all.at[1], local_sem.at[1])
    own_inv.start()
    own_div.start()

    for slot in range(listed):
        p, k = slot // slots_row, slot % slots_row
        key = jnp.where(k < count_ref[p], owner_ref[p, k] * vel_rows + local_ref[p, k], -1)
        packet[0, slot] = key
    for v in range(vel_rows):
        for column in range(3 * vel_rows):
            found = jnp.int32(-1)
            for m in range(inv_slots):
                found = jnp.where(
                    (cols_ref[v, m] == column) & (m < inv_count_ref[v]), m, found
                )
            packet[0, listed + v * 3 * vel_rows + column] = found
    packet_used = listed + 3 * vel_rows * vel_rows

    pl.semaphore_wait(barrier, owners + 1)

    def meta_copy(step, target, slot):
        return pltpu.make_async_remote_copy(
            src_ref=packet,
            dst_ref=meta.at[pl.ds(slot, 1)],
            send_sem=meta_send.at[step],
            recv_sem=meta_recv.at[step],
            device_id=target,
            device_id_type=MESH,
        )

    def send_meta(step, carry):
        meta_copy(step, ((row + step) % owners, col), row).start()
        return carry

    def piece(owner, v, first, length):
        return inv_all.at[pl.ds((owner * vel_rows + v) * inv_slots + first, length)]

    def link(index, src, dst, dy, dx):
        return pltpu.make_async_remote_copy(
            src_ref=src,
            dst_ref=dst,
            send_sem=inv_send.at[index],
            recv_sem=inv_recv.at[index],
            device_id=(at(dy, dx), col),
            device_id_type=MESH,
        )

    def move(v, along_y, amount):
        return (amount, 0) if along_y else (0, amount)

    def number(v, stage, kind):
        return (v * 5 + stage) * 4 + kind

    lines = (0, -1, 1, 2)

    def line_owner(v, stage, along_y, second):
        if stage == 0:
            dy, dx = move(v, along_y, second)
        else:
            q = lines[stage - 1]
            dy, dx = (second, q) if along_y else (q, second)
        return at(dy, dx)

    def copies(v, stage):
        first_y = v == 1
        along_y = first_y if stage == 0 else not first_y
        longer = (inv_slots + 1) // 2 if (stage + v) % 2 == 0 else inv_slots // 2
        full = (0, inv_slots)
        parts = ((1, 0, full), (-1, 0, full), (1, -1, (0, longer)), (-1, 1, (longer, inv_slots - longer)))
        made = []
        for kind, (step, source, (first, length)) in enumerate(parts):
            dy, dx = move(v, along_y, step)
            here = line_owner(v, stage, along_y, source)
            index = number(v, stage, kind)
            if stage <= 1 and kind < 2:
                outgoing = inv_ref.at[pl.ds(v * inv_slots, inv_slots)]
            else:
                outgoing = piece(here, v, first, length)
            send = link(index, outgoing, piece(here, v, first, length), dy, dx)
            coming = line_owner(v, stage, along_y, source - step)
            arriving = piece(coming, v, first, length)
            recv = link(index, arriving, arriving, dy, dx)
            made.append((send, recv))
        return made

    table = {(v, stage): copies(v, stage) for v in range(vel_rows) for stage in range(5)}

    def start(v, stage, *kinds):
        for kind in kinds:
            table[v, stage][kind][0].start()

    def arrive(v, stage, *kinds):
        for kind in kinds:
            table[v, stage][kind][1].wait_recv()

    both = range(vel_rows)
    for v in both:
        start(v, 0, 0, 1)
    lax.fori_loop(1, owners, send_meta, 0)
    meta_next = meta_copy(0, (row, nxt), owners)
    meta_prev = meta_copy(owners, (row, prv), owners + 1)
    meta_next.start()
    meta_prev.start()
    div_next = pltpu.make_async_remote_copy(
        src_ref=div_ref,
        dst_ref=div_all.at[0],
        send_sem=div_send.at[0],
        recv_sem=div_recv.at[0],
        device_id=(row, nxt),
        device_id_type=MESH,
    )
    div_prev = pltpu.make_async_remote_copy(
        src_ref=div_ref,
        dst_ref=div_all.at[2],
        send_sem=div_send.at[1],
        recv_sem=div_recv.at[1],
        device_id=(row, prv),
        device_id_type=MESH,
    )
    div_next.start()
    div_prev.start()
    for v in both:
        start(v, 1, 0, 1)

    def fill_meta(index, carry):
        meta[row, index] = packet[0, index]
        return carry

    lax.fori_loop(0, packet_used, fill_meta, 0)
    own_inv.wait()
    own_div.wait()

    for v in both:
        arrive(v, 0, 0)
        start(v, 0, 2)
        start(v, 2, 0, 1)
        arrive(v, 0, 1)
        start(v, 0, 3)
        start(v, 3, 0, 1)

    def left_part(p, carry):
        for k in range(slots_row):
            high, low = halves(div_all[1, p * slots_row + k])
            left_parts[p, :, k * side : (k + 1) * side] = high
            left_parts[p, :, (slots_row + k) * side : (slots_row + k + 1) * side] = low
        return carry

    lax.fori_loop(0, rows, left_part, 0)

    def take_meta(step, carry):
        meta_copy(step, ((row + step) % owners, col), (row + owners - step) % owners).wait_recv()
        return carry

    lax.fori_loop(1, owners, take_meta, 0)
    meta_copy(0, (row, nxt), owners).wait_recv()
    meta_copy(owners, (row, prv), owners + 1).wait_recv()
    div_next.wait_recv()
    div_prev.wait_recv()

    for v in both:
        arrive(v, 1, 0)
        start(v, 1, 2)
        arrive(v, 1, 1)
        start(v, 1, 3)

    def right_part(slot, carry):
        p = slot // slots_row
        key = packet[0, slot]
        live = key >= 0
        key = jnp.maximum(key, 0)
        owner, v = key // vel_rows, key % vel_rows
        for t, (shift, device, keys_at) in enumerate(
            ((1, 1, row), (1, 1, row), (2, 2, owners + 1), (0, 0, owners))
        ):
            base = (pattern_ref[p, t] % rows) * slots_row
            for u in range(vel_rows):
                column = shift * vel_rows + u
                place = meta[owner, listed + v * 3 * vel_rows + column]
                wanted = owner * vel_rows + u
                first, second = jnp.int32(-1), jnp.int32(-1)
                for l in range(slots_row):
                    hit = meta[keys_at, base + l] == wanted
                    second = jnp.where(hit, first, second)
                    first = jnp.where(hit, l, first)
                good = live & (t < pattern_count_ref[p]) & (place >= 0)
                one = jnp.where(good & (first >= 0), 1.0, 0.0)
                two = jnp.where(good & (second >= 0), 1.0, 0.0)
                value = (
                    one * div_all[device, base + jnp.maximum(first, 0)]
                    + two * div_all[device, base + jnp.maximum(second, 0)]
                )
                high, low = halves(value)
                lines_at = pl.ds(t * side, side)
                right_parts[slot, lines_at, u * side : (u + 1) * side] = high
                right_parts[slot, lines_at, (vel_rows + u) * side : (vel_rows + u + 1) * side] = low
                if t != 1:
                    places[slot, column] = key * inv_slots + jnp.maximum(place, 0)
        return carry

    lax.fori_loop(0, listed, right_part, 0)

    for v in both:
        arrive(v, 0, 2, 3)
        start(v, 4, 0, 1)
    for stage in (2, 3):
        for v in both:
            arrive(v, stage, 0)
            start(v, stage, 2)
            arrive(v, stage, 1)
            start(v, stage, 3)
    for v in both:
        arrive(v, 4, 0)
        start(v, 4, 2)
        arrive(v, 4, 1)
        start(v, 4, 3)
    for stage in (1, 2, 3, 4):
        for v in both:
            arrive(v, stage, 2, 3)

    width = vel_rows * side

    def answer(p, carry):
        def one_slot(k, inner):
            slot = p * slots_row + k
            for shift, t, wide in ((0, 3, 1), (1, 0, 2), (2, 2, 1)):
                blocks = [
                    halves(inv_all[places[slot, shift * vel_rows + u]]) for u in range(vel_rows)
                ]
                high = jnp.concatenate([b[0] for b in blocks], axis=1)
                low = jnp.concatenate([b[1] for b in blocks], axis=1)
                given = right_parts[slot, t * side : (t + wide) * side, :]
                given_high, given_low = given[:, :width], given[:, width:]
                product = lax.dot_general(
                    jnp.concatenate([high, high, low], axis=1),
                    jnp.concatenate([given_high, given_low, given_high], axis=1),
                    (((1,), (1,)), ((), ())),
                    preferred_element_type=F32,
                )
                product_high, product_low = halves(product)
                here = pl.ds(pl.multiple_of(k * side, side), side)
                factors[0, here, t * side : (t + wide) * side] = product_high
                factors[1, here, t * side : (t + wide) * side] = product_low
            return inner

        lax.fori_loop(0, slots_row, one_slot, 0)
        depth = slots_row * side
        left_high = left_parts[p, :, :depth]
        left_low = left_parts[p, :, depth:]
        result = (
            jnp.dot(left_high, factors[0], preferred_element_type=F32)
            + jnp.dot(left_high, factors[1], preferred_element_type=F32)
            + jnp.dot(left_low, factors[0], preferred_element_type=F32)
        )
        for t in range(pattern):
            out_ref[p, t] = result[:, t * side : (t + 1) * side]
        return carry

    lax.fori_loop(0, rows, answer, 0)

    def sent_meta(step, carry):
        meta_copy(step, ((row + step) % owners, col), row).wait_send()
        return carry

    lax.fori_loop(1, owners, sent_meta, 0)
    meta_next.wait_send()
    meta_prev.wait_send()
    div_next.wait_send()
    div_prev.wait_send()
    for pairs in table.values():
        for send, _ in pairs:
            send.wait_send()


def local(
    lon_count,
    div_blocks,
    div_owner,
    div_local,
    div_count,
    inv_blocks,
    inv_cols,
    inv_count,
    schur_cols,
    schur_count,
):
    rows, slots_row, side, _ = div_blocks.shape
    vel_rows, inv_slots = inv_cols.shape
    pattern = schur_cols.shape[1]
    listed = rows * slots_row
    owners = SIDE * SIDE
    smem = pl.BlockSpec(memory_space=pltpu.SMEM)
    anywhere = pl.BlockSpec(memory_space=pl.ANY)
    return pl.pallas_call(
        functools.partial(kernel, lon_count),
        out_shape=jax.ShapeDtypeStruct((rows, pattern, side, side), F32),
        in_specs=[smem] * 7 + [anywhere] * 2,
        out_specs=pl.BlockSpec(memory_space=pltpu.VMEM),
        scratch_shapes=[
            pltpu.VMEM((owners * vel_rows * inv_slots, side, side), F32),
            pltpu.VMEM((3, listed, side, side), F32),
            pltpu.VMEM((listed, pattern * side, 2 * vel_rows * side), BF16),
            pltpu.VMEM((rows, side, 2 * slots_row * side), BF16),
            pltpu.VMEM((2, slots_row * side, pattern * side), BF16),
            pltpu.SMEM((1, 128), jnp.int32),
            pltpu.SMEM((owners + 2, 128), jnp.int32),
            pltpu.SMEM((listed, 3 * vel_rows), jnp.int32),
            pltpu.SemaphoreType.DMA((2,)),
            pltpu.SemaphoreType.DMA((2,)),
            pltpu.SemaphoreType.DMA((2,)),
            pltpu.SemaphoreType.DMA((owners + 1,)),
            pltpu.SemaphoreType.DMA((owners + 1,)),
            pltpu.SemaphoreType.DMA((40,)),
            pltpu.SemaphoreType.DMA((40,)),
        ],
        compiler_params=pltpu.CompilerParams(
            collective_id=0, has_side_effects=True, vmem_limit_bytes=40 * 2**20
        ),
    )(
        div_owner,
        div_local,
        div_count,
        inv_cols,
        inv_count,
        schur_cols,
        schur_count,
        div_blocks.reshape(listed, side, side),
        inv_blocks.reshape(vel_rows * inv_slots, side, side),
    )


def solution(mesh):
    placed = (
        P(("row", "col"), None, None, None),
        P(("row", "col"), None),
        P(("row", "col"), None),
        P(("row", "col")),
        P(("row", "col"), None, None, None),
        P(("row", "col"), None),
        P(("row", "col")),
        P(("row", "col"), None),
        P(("row", "col")),
    )
    return jax.shard_map(
        functools.partial(local, mesh.shape["col"]),
        mesh=mesh,
        in_specs=placed,
        out_specs=P(("row", "col"), None, None, None),
        check_vma=False,
    )
```

```python
import functools

import jax
import jax.numpy as jnp
from jax import lax
from jax.experimental import pallas as pl
from jax.experimental.pallas import tpu as pltpu
from jax.sharding import PartitionSpec as P

MESH = pl.DeviceIdType.MESH
F32 = jnp.float32
BF16 = jnp.bfloat16
SIDE = 4
CLASS = 8
META_WIDTH = 128


def halves(value):
    high = value.astype(BF16)
    return high, (value - high.astype(F32)).astype(BF16)


def kernel(
    lon_count,
    owner_hbm,
    local_hbm,
    count_hbm,
    cols_hbm,
    inv_count_hbm,
    pattern_hbm,
    pattern_count_hbm,
    div_ref,
    inv_ref,
    out_ref,
    inv_all,
    div_own,
    div_mate,
    div_pass,
    right_parts,
    left_parts,
    factors,
    mate_sum,
    given_sum,
    packet,
    meta,
    places,
    owner_ref,
    local_ref,
    count_ref,
    cols_ref,
    inv_count_ref,
    pattern_ref,
    pattern_count_ref,
    local_sem,
    div_send,
    div_recv,
    meta_send,
    meta_recv,
    inv_send,
    inv_recv,
    sum_send,
    sum_recv,
):
    rows, slots_row = owner_ref.shape
    vel_rows, inv_slots = cols_ref.shape
    pattern = pattern_ref.shape[1]
    listed = rows * slots_row
    columns = 3 * vel_rows
    side = out_ref.shape[2]
    row = lax.axis_index("row")
    col = lax.axis_index("col")
    odd = col % 2
    nxt = (col + 1) % lon_count
    prv = (col + lon_count - 1) % lon_count
    step_u = 1 + (SIDE - 1) * odd
    step_w = SIDE - (SIDE - 1) * odd
    u = (row // step_u) % SIDE
    w = (row // step_w) % SIDE
    half = u // 2

    def at(u_at, w_at):
        return u_at * step_u + w_at * step_w

    def ring(amount):
        return (w + amount + SIDE) % SIDE

    mate_row = at(u + 1 - 2 * (u % 2), w)
    other_row = at(u, w + 1 - 2 * (w % 2))
    across = at(SIDE - 1 - u, w)

    small = [
        pltpu.make_async_copy(src, dst, local_sem.at[i])
        for i, (src, dst) in enumerate(
            (
                (owner_hbm, owner_ref),
                (local_hbm, local_ref),
                (count_hbm, count_ref),
                (cols_hbm, cols_ref),
                (inv_count_hbm, inv_count_ref),
                (pattern_hbm, pattern_ref),
                (pattern_count_hbm, pattern_count_ref),
            )
        )
    ]
    for copy in small:
        copy.start()
    mine = w * 2 + half
    piece_rows = vel_rows * inv_slots
    own_inv = pltpu.make_async_copy(
        inv_ref, inv_all.at[pl.ds(mine * piece_rows, piece_rows)], local_sem.at[7]
    )
    own_div = pltpu.make_async_copy(div_ref, div_own.at[pl.ds(0, listed)], local_sem.at[8])
    own_inv.start()
    own_div.start()

    kin = [(at(u, ring(k)), col) for k in (1, 2, 3)]
    kin += [(at(SIDE - 1 - u, ring(k)), col) for k in (0, 1, 2, 3)]
    near = [(mate_row, col), (row, nxt), (row, prv), (other_row, nxt), (other_row, prv)]
    heard = [(mate_row, nxt), (mate_row, prv)]
    barrier = pltpu.get_barrier_semaphore()
    for peer in kin + near + heard:
        pl.semaphore_signal(barrier, inc=1, device_id=peer, device_id_type=MESH)

    for copy in small:
        copy.wait()
    inv_at = listed
    pattern_at = inv_at + vel_rows * columns
    used = pattern_at + rows * pattern
    own_key = CLASS

    def note(place, value):
        packet[0, place] = value
        meta[mine, place] = value
        meta[own_key, place] = value

    for slot in range(listed):
        p, k = slot // slots_row, slot % slots_row
        note(slot, jnp.where(k < count_ref[p], owner_ref[p, k] * vel_rows + local_ref[p, k], -1))
    for v in range(vel_rows):
        for column in range(columns):
            found = jnp.int32(-1)
            for m in range(inv_slots):
                hit = (cols_ref[v, m] == column) & (m < inv_count_ref[v])
                found = jnp.where(hit, m, found)
            note(inv_at + v * columns + column, found)
    for p in range(rows):
        for t in range(pattern):
            note(
                pattern_at + p * pattern + t,
                jnp.where(t < pattern_count_ref[p], pattern_ref[p, t] % rows, -1),
            )

    pl.semaphore_wait(barrier, len(kin + near + heard))

    sends = []

    def remote(src, dst, send, recv, target):
        return pltpu.make_async_remote_copy(
            src_ref=src,
            dst_ref=dst,
            send_sem=send,
            recv_sem=recv,
            device_id=target,
            device_id_type=MESH,
        )

    meta_rows = [mine] * 7 + [own_key + 3, own_key + 1, own_key + 2, own_key + 4, own_key + 5]
    from_rows = [ring(-k) * 2 + half for k in (1, 2, 3)]
    from_rows += [ring(-k) * 2 + (1 - half) for k in (0, 1, 2, 3)]
    from_rows += meta_rows[7:]
    meta_in = []
    for i, peer in enumerate(kin + near):
        send = remote(
            packet, meta.at[pl.ds(meta_rows[i], 1)], meta_send.at[i], meta_recv.at[i], peer
        )
        send.start()
        sends.append(send)
        arrived = meta.at[pl.ds(from_rows[i], 1)]
        meta_in.append(remote(packet, arrived, meta_send.at[i], meta_recv.at[i], peer))

    def piece(w_at, b, v, first, length):
        return inv_all.at[pl.ds((w_at * 2 + b) * piece_rows + v * inv_slots + first, length)]

    made = []

    def exchange(outgoing, placed, coming, target):
        index = len(made)
        send = remote(outgoing, placed, inv_send.at[index], inv_recv.at[index], (target, col))
        recv = remote(coming, coming, inv_send.at[index], inv_recv.at[index], (target, col))
        made.append(send)
        return send, recv

    def own_piece(v):
        return inv_ref.at[pl.ds(v * inv_slots, inv_slots)]

    def ring_copies(v, b, source, cut):
        copies = []
        for way in (1, -1):
            copies.append(
                exchange(
                    source,
                    piece(w, b, v, 0, inv_slots),
                    piece(ring(-way), b, v, 0, inv_slots),
                    at(u, ring(way)),
                )
            )
        for way, first, length in ((1, 0, cut), (-1, cut, inv_slots - cut)):
            passed = piece(ring(-way), b, v, first, length)
            copies.append(
                exchange(
                    passed, passed, piece(ring(-2 * way), b, v, first, length), at(u, ring(way))
                )
            )
        return copies

    def cross_copy(v, amount, source, first, length):
        given = piece(ring(amount), half, v, first, length) if source is None else source
        return exchange(
            given,
            piece(ring(amount), half, v, first, length),
            piece(ring(amount), 1 - half, v, first, length),
            across,
        )

    cut = (inv_slots + 1) // 2
    cross_first = cross_copy(0, 0, own_piece(0), 0, inv_slots)
    ring_own = ring_copies(0, half, own_piece(0), cut)
    ring_far = ring_copies(0, 1 - half, piece(w, 1 - half, 0, 0, inv_slots), inv_slots - cut)
    ring_last = ring_copies(1, half, own_piece(1), cut)
    cross_last = [
        cross_copy(1, 0, own_piece(1), 0, inv_slots),
        cross_copy(1, -1, None, 0, inv_slots),
        cross_copy(1, 1, None, 0, inv_slots),
        cross_copy(1, 2, None, 0, cut),
        cross_copy(1, 2, None, cut, inv_slots - cut),
    ]

    def start(pair):
        pair[0].start()

    def arrive(pair):
        pair[1].wait_recv()

    def blocks(buffer, third):
        return buffer.at[pl.ds(third * listed, listed)]

    div_plan = [
        (div_ref, div_pass, (other_row, col)),
        (div_ref, blocks(div_mate, 0), (mate_row, col)),
        (div_ref, blocks(div_own, 1), (row, nxt)),
        (div_ref, blocks(div_own, 2), (row, prv)),
        (div_pass, blocks(div_mate, 1), (row, nxt)),
        (div_pass, blocks(div_mate, 2), (row, prv)),
    ]
    div_copies = [
        remote(src, dst, div_send.at[i], div_recv.at[i], peer)
        for i, (src, dst, peer) in enumerate(div_plan)
    ]

    start(cross_first)
    start(ring_last[0])
    start(ring_last[1])
    for copy in div_copies[:4]:
        copy.start()
    start(ring_own[0])
    start(ring_own[1])
    start(cross_last[0])
    own_inv.wait()
    own_div.wait()

    arrive(cross_first)
    start(ring_far[0])
    start(ring_far[1])
    arrive(ring_last[0])
    start(ring_last[2])
    start(cross_last[1])
    arrive(ring_last[1])
    start(ring_last[3])
    start(cross_last[2])

    def left_part(group, source):
        def one(p, carry):
            for k in range(slots_row):
                high, low = halves(source[p * slots_row + k])
                left_parts[group, p, :, k * side : (k + 1) * side] = high
                left_parts[group, p, :, (slots_row + k) * side : (slots_row + k + 1) * side] = low
            return carry

        lax.fori_loop(0, rows, one, 0)

    left_part(0, div_own)
    for copy in meta_in:
        copy.wait_recv()

    arrive(ring_own[0])
    start(ring_own[2])
    arrive(ring_own[1])
    start(ring_own[3])
    div_copies[0].wait_recv()
    div_copies[4].start()
    div_copies[5].start()
    div_copies[2].wait_recv()
    div_copies[3].wait_recv()

    def right_part(group, source):
        keys_own = own_key + 3 * group

        def one(slot, carry):
            p = slot // slots_row
            key = meta[keys_own, slot]
            live = key >= 0
            key = jnp.maximum(key, 0)
            owner, v = key // vel_rows, key % vel_rows
            owner_y, owner_x = owner // SIDE, owner % SIDE
            owner_u = owner_x + odd * (owner_y - owner_x)
            owner_w = owner_y + odd * (owner_x - owner_y)
            live = live & (((owner_u + 1) // 2) % 2 == ((u + 1) // 2) % 2)
            found = owner_w * 2 + owner_u // 2
            for t, (shift, third) in enumerate(((1, 0), (1, 0), (2, 2), (0, 1))):
                wanted_row = meta[keys_own, pattern_at + p * pattern + t]
                chosen = live & (wanted_row >= 0)
                base = jnp.maximum(wanted_row, 0) * slots_row
                for c in range(vel_rows):
                    column = shift * vel_rows + c
                    place = meta[found, inv_at + v * columns + column]
                    wanted = owner * vel_rows + c
                    first, second = jnp.int32(-1), jnp.int32(-1)
                    for l in range(slots_row):
                        hit = meta[keys_own + third, base + l] == wanted
                        second = jnp.where(hit, first, second)
                        first = jnp.where(hit, l, first)
                    good = chosen & (place >= 0)
                    one_on = jnp.where(good & (first >= 0), 1.0, 0.0)
                    two_on = jnp.where(good & (second >= 0), 1.0, 0.0)
                    here = third * listed + base
                    value = (
                        one_on * source[here + jnp.maximum(first, 0)]
                        + two_on * source[here + jnp.maximum(second, 0)]
                    )
                    high, low = halves(value)
                    lines = pl.ds(t * side, side)
                    at_slot = group * listed + slot
                    right_parts[at_slot, lines, c * side : (c + 1) * side] = high
                    right_parts[
                        at_slot, lines, (vel_rows + c) * side : (vel_rows + c + 1) * side
                    ] = low
                    if t != 1:
                        places[at_slot, column] = (
                            found * piece_rows + v * inv_slots + jnp.maximum(place, 0)
                        )
            return carry

        lax.fori_loop(0, listed, one, 0)

    right_part(0, div_own)

    arrive(ring_last[2])
    start(cross_last[3])
    arrive(ring_last[3])
    start(cross_last[4])
    arrive(ring_far[0])
    start(ring_far[2])
    arrive(ring_far[1])
    start(ring_far[3])

    div_copies[1].wait_recv()
    div_copies[4].wait_recv()
    div_copies[5].wait_recv()
    left_part(1, div_mate)
    right_part(1, div_mate)

    for pair in (*ring_own[2:], *cross_last, *ring_far[2:]):
        arrive(pair)

    width = vel_rows * side

    def answer(group, p, target):
        def one_slot(k, carry):
            slot = group * listed + p * slots_row + k
            for shift, t, wide in ((0, 3, 1), (1, 0, 2), (2, 2, 1)):
                parts = [halves(inv_all[places[slot, shift * vel_rows + c]]) for c in range(vel_rows)]
                high = jnp.concatenate([part[0] for part in parts], axis=1)
                low = jnp.concatenate([part[1] for part in parts], axis=1)
                given = right_parts[slot, t * side : (t + wide) * side, :]
                given_high, given_low = given[:, :width], given[:, width:]
                product = lax.dot_general(
                    jnp.concatenate([high, high, low], axis=1),
                    jnp.concatenate([given_high, given_low, given_high], axis=1),
                    (((1,), (1,)), ((), ())),
                    preferred_element_type=F32,
                )
                product_high, product_low = halves(product)
                here = pl.ds(pl.multiple_of(k * side, side), side)
                factors[0, here, t * side : (t + wide) * side] = product_high
                factors[1, here, t * side : (t + wide) * side] = product_low
            return carry

        lax.fori_loop(0, slots_row, one_slot, 0)
        depth = slots_row * side
        left_high = left_parts[group, p, :, :depth]
        left_low = left_parts[group, p, :, depth:]
        result = (
            jnp.dot(left_high, factors[0], preferred_element_type=F32)
            + jnp.dot(left_high, factors[1], preferred_element_type=F32)
            + jnp.dot(left_low, factors[0], preferred_element_type=F32)
        )
        for t in range(pattern):
            target[p, t] = result[:, t * side : (t + 1) * side]

    returns = [
        remote(
            mate_sum.at[pl.ds(p, 1)],
            given_sum.at[pl.ds(p, 1)],
            sum_send.at[p],
            sum_recv.at[p],
            (mate_row, col),
        )
        for p in range(rows)
    ]
    for p in range(rows):
        answer(1, p, mate_sum)
        returns[p].start()
    for p in range(rows):
        answer(0, p, out_ref)
    for p in range(rows):
        returns[p].wait_recv()
        out_ref[p] = out_ref[p] + given_sum[p]

    for copy in (*sends, *div_copies, *made, *returns):
        copy.wait_send()


def local(
    lon_count,
    div_blocks,
    div_owner,
    div_local,
    div_count,
    inv_blocks,
    inv_cols,
    inv_count,
    schur_cols,
    schur_count,
):
    rows, slots_row, side, _ = div_blocks.shape
    vel_rows, inv_slots = inv_cols.shape
    pattern = schur_cols.shape[1]
    listed = rows * slots_row
    width = pattern * side
    ints = (div_owner, div_local, div_count, inv_cols, inv_count, schur_cols, schur_count)
    operands = [
        pltpu.with_memory_space_constraint(value, pltpu.HBM)
        for value in (
            *ints,
            div_blocks.reshape(listed, side, side),
            inv_blocks.reshape(vel_rows * inv_slots, side, side),
        )
    ]
    return pl.pallas_call(
        functools.partial(kernel, lon_count),
        out_shape=jax.ShapeDtypeStruct((rows, pattern, side, side), F32),
        in_specs=[pl.BlockSpec(memory_space=pltpu.HBM)] * len(operands),
        out_specs=pl.BlockSpec(memory_space=pltpu.VMEM),
        scratch_shapes=[
            pltpu.VMEM((CLASS * vel_rows * inv_slots, side, side), F32),
            pltpu.VMEM((3 * listed, side, side), F32),
            pltpu.VMEM((3 * listed, side, side), F32),
            pltpu.VMEM((listed, side, side), F32),
            pltpu.VMEM((2 * listed, width, 2 * vel_rows * side), BF16),
            pltpu.VMEM((2, rows, side, 2 * slots_row * side), BF16),
            pltpu.VMEM((2, slots_row * side, width), BF16),
            pltpu.VMEM((rows, pattern, side, side), F32),
            pltpu.VMEM((rows, pattern, side, side), F32),
            pltpu.SMEM((1, META_WIDTH), jnp.int32),
            pltpu.SMEM((CLASS + 6, META_WIDTH), jnp.int32),
            pltpu.SMEM((2 * listed, 3 * vel_rows), jnp.int32),
            *[pltpu.SMEM(value.shape, jnp.int32) for value in ints],
            pltpu.SemaphoreType.DMA((9,)),
            pltpu.SemaphoreType.DMA((6,)),
            pltpu.SemaphoreType.DMA((6,)),
            pltpu.SemaphoreType.DMA((12,)),
            pltpu.SemaphoreType.DMA((12,)),
            pltpu.SemaphoreType.DMA((18,)),
            pltpu.SemaphoreType.DMA((18,)),
            pltpu.SemaphoreType.DMA((rows,)),
            pltpu.SemaphoreType.DMA((rows,)),
        ],
        compiler_params=pltpu.CompilerParams(
            collective_id=0, has_side_effects=True, vmem_limit_bytes=56 * 2**20
        ),
    )(*operands)


def solution(mesh):
    placed = (
        P(("row", "col"), None, None, None),
        P(("row", "col"), None),
        P(("row", "col"), None),
        P(("row", "col")),
        P(("row", "col"), None, None, None),
        P(("row", "col"), None),
        P(("row", "col")),
        P(("row", "col"), None),
        P(("row", "col")),
    )
    return jax.shard_map(
        functools.partial(local, mesh.shape["col"]),
        mesh=mesh,
        in_specs=placed,
        out_specs=P(("row", "col"), None, None, None),
        check_vma=False,
    )
```

```python
import functools

import jax
import jax.numpy as jnp
from jax import lax
from jax.experimental import pallas as pl
from jax.experimental.pallas import tpu as pltpu
from jax.sharding import PartitionSpec as P

MESH = pl.DeviceIdType.MESH
F32 = jnp.float32
BF16 = jnp.bfloat16
SIDE = 4
CLASS = 8
META_WIDTH = 128


def halves(value):
    high = value.astype(BF16)
    return high, (value - high.astype(F32)).astype(BF16)


def kernel(
    lon_count,
    owner_hbm,
    local_hbm,
    count_hbm,
    cols_hbm,
    inv_count_hbm,
    pattern_hbm,
    pattern_count_hbm,
    div_ref,
    inv_ref,
    out_ref,
    *scratch,
):
    held = scratch[:CLASS]
    (
        div_own,
        div_own_side,
        div_mate,
        div_mate_side,
        div_pass,
        dense_div,
        dense_inv,
        sums,
        given,
        packet,
        meta,
        owner_ref,
        local_ref,
        count_ref,
        cols_ref,
        inv_count_ref,
        pattern_ref,
        pattern_count_ref,
        local_sem,
        div_send,
        div_recv,
        meta_send,
        meta_recv,
        inv_send,
        inv_recv,
        sum_send,
        sum_recv,
    ) = scratch[CLASS:]
    rows, slots_row = owner_ref.shape
    vel_rows, inv_slots = cols_ref.shape
    pattern = pattern_ref.shape[1]
    listed = rows * slots_row
    columns = 3 * vel_rows
    side = out_ref.shape[2]
    width = vel_rows * side
    row = lax.axis_index("row")
    col = lax.axis_index("col")
    odd = col % 2
    nxt = (col + 1) % lon_count
    prv = (col + lon_count - 1) % lon_count
    step_u = 1 + (SIDE - 1) * odd
    step_w = SIDE - (SIDE - 1) * odd
    u = (row // step_u) % SIDE
    w = (row // step_w) % SIDE

    def at(u_at, w_at):
        return u_at * step_u + w_at * step_w

    def ring(amount):
        return (w + amount + SIDE) % SIDE

    mate_row = at(u + 1 - 2 * (u % 2), w)
    other_row = at(u, w + 1 - 2 * (w % 2))
    across = at(SIDE - 1 - u, w)

    small = [
        pltpu.make_async_copy(src, dst, local_sem.at[i])
        for i, (src, dst) in enumerate(
            (
                (owner_hbm, owner_ref),
                (local_hbm, local_ref),
                (count_hbm, count_ref),
                (cols_hbm, cols_ref),
                (inv_count_hbm, inv_count_ref),
                (pattern_hbm, pattern_ref),
                (pattern_count_hbm, pattern_count_ref),
            )
        )
    ]
    for copy in small:
        copy.start()
    own_inv = pltpu.make_async_copy(inv_ref, held[0], local_sem.at[7])
    own_div = pltpu.make_async_copy(div_ref, div_own, local_sem.at[8])
    own_inv.start()
    own_div.start()

    kin = [(at(u, ring(k)), col) for k in (1, 2, 3)]
    kin += [(at(SIDE - 1 - u, ring(k)), col) for k in (0, 1, 2, 3)]
    near = [(mate_row, col), (row, nxt), (row, prv), (other_row, nxt), (other_row, prv)]
    heard = [(mate_row, nxt), (mate_row, prv)]
    barrier = pltpu.get_barrier_semaphore()
    for peer in kin + near + heard:
        pl.semaphore_signal(barrier, inc=1, device_id=peer, device_id_type=MESH)

    for copy in small:
        copy.wait()
    inv_at = listed
    pattern_at = inv_at + vel_rows * columns
    own_key = CLASS

    def note(place, value):
        packet[0, place] = value
        meta[0, place] = value
        meta[own_key, place] = value

    for slot in range(listed):
        p, k = slot // slots_row, slot % slots_row
        note(slot, jnp.where(k < count_ref[p], owner_ref[p, k] * vel_rows + local_ref[p, k], -1))
    for v in range(vel_rows):
        for column in range(columns):
            found = jnp.int32(-1)
            for m in range(inv_slots):
                hit = (cols_ref[v, m] == column) & (m < inv_count_ref[v])
                found = jnp.where(hit, m, found)
            note(inv_at + v * columns + column, found)
    for p in range(rows):
        for t in range(pattern):
            note(pattern_at + p * pattern + t, pattern_ref[p, t] % rows)

    pl.semaphore_wait(barrier, len(kin + near + heard))

    def remote(src, dst, send, recv, target):
        return pltpu.make_async_remote_copy(
            src_ref=src,
            dst_ref=dst,
            send_sem=send,
            recv_sem=recv,
            device_id=target,
            device_id_type=MESH,
        )

    def piece(offset, b, v, first, length):
        return held[(offset % SIDE) * 2 + b].at[pl.ds(v * inv_slots + first, length)]

    made = []

    def exchange(outgoing, placed, target):
        index = len(made)
        copy = remote(outgoing, placed, inv_send.at[index], inv_recv.at[index], (target, col))
        made.append(copy)
        return copy

    def own_piece(v):
        return inv_ref.at[pl.ds(v * inv_slots, inv_slots)]

    def ring_copies(v, b, source, cut):
        copies = []
        for way in (1, -1):
            copies.append(
                exchange(source, piece(-way, b, v, 0, inv_slots), at(u, ring(way)))
            )
        for way, first, length in ((1, 0, cut), (-1, cut, inv_slots - cut)):
            copies.append(
                exchange(
                    piece(-way, b, v, first, length),
                    piece(2, b, v, first, length),
                    at(u, ring(way)),
                )
            )
        return copies

    def cross_copy(v, offset, first, length):
        outgoing = own_piece(v) if offset == 0 else piece(offset, 0, v, first, length)
        return exchange(outgoing, piece(offset, 1, v, first, length), across)

    cut = (inv_slots + 1) // 2
    cross_first = cross_copy(0, 0, 0, inv_slots)
    ring_own = ring_copies(0, 0, own_piece(0), cut)
    ring_far = ring_copies(0, 1, piece(0, 1, 0, 0, inv_slots), inv_slots - cut)
    ring_last = ring_copies(1, 0, own_piece(1), cut)
    cross_last = [
        cross_copy(1, 0, 0, inv_slots),
        cross_copy(1, -1, 0, inv_slots),
        cross_copy(1, 1, 0, inv_slots),
        cross_copy(1, 2, 0, cut),
        cross_copy(1, 2, cut, inv_slots - cut),
    ]

    plan = []
    for part in range(2):
        some = pl.ds(part * slots_row, slots_row)
        plan.append((div_ref.at[some], div_pass.at[some], (other_row, col)))
    plan += [
        (div_ref, div_own_side.at[pl.ds(0, listed)], (row, nxt)),
        (div_ref, div_own_side.at[pl.ds(listed, listed)], (row, prv)),
        (div_ref, div_mate, (mate_row, col)),
    ]
    for part in range(2):
        some = pl.ds(part * slots_row, slots_row)
        for third, target in ((1, nxt), (2, prv)):
            there = pl.ds((third - 1) * listed + part * slots_row, slots_row)
            plan.append((div_pass.at[some], div_mate_side.at[there], (row, target)))
    div_copies = [
        remote(src, dst, div_send.at[i], div_recv.at[i], peer)
        for i, (src, dst, peer) in enumerate(plan)
    ]

    meta_rows = [((-k) % SIDE) * 2 for k in (1, 2, 3)]
    meta_rows += [((-k) % SIDE) * 2 + 1 for k in (0, 1, 2, 3)]
    meta_rows += [own_key + 3, own_key + 1, own_key + 2, own_key + 4, own_key + 5]
    meta_copies = [
        remote(packet, meta.at[pl.ds(meta_rows[i], 1)], meta_send.at[i], meta_recv.at[i], peer)
        for i, peer in enumerate(kin + near)
    ]

    div_copies[0].start()
    div_copies[1].start()
    cross_first.start()
    ring_last[0].start()
    ring_last[1].start()
    for copy in meta_copies:
        copy.start()
    div_copies[2].start()
    div_copies[3].start()
    ring_own[0].start()
    ring_own[1].start()
    cross_last[0].start()
    sums[...] = jnp.zeros_like(sums)
    own_inv.wait()
    own_div.wait()

    def spread(group, thirds):
        keys_own = own_key + 3 * group
        home, beside = ((div_own, div_own_side), (div_mate, div_mate_side))[group]

        def one(rel, carry):
            owner_u = u + (rel % 2) * (SIDE - 1 - 2 * u)
            owner = at(owner_u, (w + rel // 2) % SIDE)
            for third in thirds:
                for p in range(rows):
                    base = p * slots_row
                    if third:
                        t = 3 if third == 1 else 2
                        base = meta[keys_own, pattern_at + p * pattern + t] * slots_row
                    for c in range(vel_rows):
                        wanted = owner * vel_rows + c
                        first, second = jnp.int32(-1), jnp.int32(-1)
                        for l in range(slots_row):
                            hit = meta[keys_own + third, base + l] == wanted
                            second = jnp.where(hit, first, second)
                            first = jnp.where(hit, l, first)
                        one_on = jnp.where(first >= 0, 1.0, 0.0)
                        two_on = jnp.where(second >= 0, 1.0, 0.0)
                        source = beside if third else home
                        here = max(third - 1, 0) * listed + base
                        value = (
                            one_on * source[here + jnp.maximum(first, 0)]
                            + two_on * source[here + jnp.maximum(second, 0)]
                        )
                        high, low = halves(value)
                        place = group * CLASS + rel
                        lines = slice(p * side, (p + 1) * side)
                        at_high = slice(c * side, (c + 1) * side)
                        at_low = slice(width + c * side, width + (c + 1) * side)
                        dense_div[place, third, lines, at_high] = high
                        dense_div[place, third, lines, at_low] = low
            return carry

        lax.fori_loop(0, CLASS, one, 0)

    def gather(rel):
        for v in range(vel_rows):
            for column in range(columns):
                place = meta[rel, inv_at + v * columns + column]
                on = jnp.where(place >= 0, 1.0, 0.0)
                high, low = halves(on * held[rel][v * inv_slots + jnp.maximum(place, 0)])
                third = (1, 0, 2)[column // vel_rows]
                c = column % vel_rows
                lines = slice(v * side, (v + 1) * side)
                dense_inv[rel, third, lines, c * side : (c + 1) * side] = high
                dense_inv[rel, third, lines, width + c * side : width + (c + 1) * side] = low

    def product(rel, group, only=None):
        place = group * CLASS + rel
        factors = []
        for third in range(3):
            inv = dense_inv[rel, third]
            div = dense_div[place, third]
            inv_high, inv_low = inv[:, :width], inv[:, width:]
            div_high, div_low = div[:, :width], div[:, width:]
            value = lax.dot_general(
                jnp.concatenate([inv_high, inv_high, inv_low], axis=1),
                jnp.concatenate([div_high, div_low, div_high], axis=1),
                (((1,), (1,)), ((), ())),
                preferred_element_type=F32,
            )
            factors.append(halves(value))
        for p in range(rows):
            order = ((0, p), (0, 1 - p), (2, p), (1, p))
            high, low = (
                jnp.concatenate(
                    [factors[third][i][:, q * side : (q + 1) * side] for third, q in order], axis=1
                )
                for i in range(2)
            )
            left = dense_div[place, 0, p * side : (p + 1) * side, :]
            left_high, left_low = left[:, :width], left[:, width:]
            sums[group, p] += jnp.dot(
                jnp.concatenate([left_high, left_high, left_low], axis=1),
                jnp.concatenate([high, low, high], axis=0),
                preferred_element_type=F32,
            )
            if only is not None:
                only[p].start()

    cross_first.wait_recv()
    ring_far[0].start()
    ring_far[1].start()
    ring_last[0].wait_recv()
    ring_last[2].start()
    cross_last[1].start()
    ring_last[1].wait_recv()
    ring_last[3].start()
    cross_last[2].start()

    spread(0, (0,))

    for part in range(2):
        div_copies[part].wait_recv()
        div_copies[5 + 2 * part].start()
        div_copies[6 + 2 * part].start()
    div_copies[4].start()
    ring_own[0].wait_recv()
    ring_own[2].start()
    ring_own[1].wait_recv()
    ring_own[3].start()
    for copy in meta_copies:
        copy.wait_recv()
    div_copies[2].wait_recv()
    div_copies[3].wait_recv()
    spread(0, (1, 2))
    ring_last[2].wait_recv()
    cross_last[3].start()
    ring_last[3].wait_recv()
    cross_last[4].start()
    gather(0)
    product(0, 0)
    ring_far[0].wait_recv()
    ring_far[2].start()
    ring_far[1].wait_recv()
    ring_far[3].start()
    cross_last[0].wait_recv()
    early = (1, 6, 2)
    for rel in early:
        gather(rel)
        product(rel, 0)
    for copy in div_copies[4:]:
        copy.wait_recv()
    spread(1, (0, 1, 2))
    for rel in (0, *early):
        product(rel, 1)
    ring_own[2].wait_recv()
    ring_own[3].wait_recv()
    gather(4)
    product(4, 0)
    product(4, 1)
    for rel, copy in ((7, cross_last[1]), (3, cross_last[2])):
        copy.wait_recv()
        gather(rel)
        product(rel, 0)
        product(rel, 1)
    for copy in (*cross_last[3:], *ring_far[2:]):
        copy.wait_recv()
    gather(5)
    returns = [
        remote(
            sums.at[1, pl.ds(p, 1)],
            given.at[pl.ds(p, 1)],
            sum_send.at[p],
            sum_recv.at[p],
            (mate_row, col),
        )
        for p in range(rows)
    ]
    product(5, 1, returns)
    product(5, 0)
    for p in range(rows):
        returns[p].wait_recv()
        total = sums[0, p] + given[p]
        for t in range(pattern):
            kept = jnp.where(t < pattern_count_ref[p], 1.0, 0.0)
            out_ref[p, t] = kept * total[:, t * side : (t + 1) * side]

    for copy in (*meta_copies, *div_copies, *made, *returns):
        copy.wait_send()


def local(
    lon_count,
    div_blocks,
    div_owner,
    div_local,
    div_count,
    inv_blocks,
    inv_cols,
    inv_count,
    schur_cols,
    schur_count,
):
    rows, slots_row, side, _ = div_blocks.shape
    vel_rows, inv_slots = inv_cols.shape
    pattern = schur_cols.shape[1]
    listed = rows * slots_row
    width = pattern * side
    ints = (div_owner, div_local, div_count, inv_cols, inv_count, schur_cols, schur_count)
    operands = [
        pltpu.with_memory_space_constraint(value, pltpu.HBM)
        for value in (
            *ints,
            div_blocks.reshape(listed, side, side),
            inv_blocks.reshape(vel_rows * inv_slots, side, side),
        )
    ]
    return pl.pallas_call(
        functools.partial(kernel, lon_count),
        out_shape=jax.ShapeDtypeStruct((rows, pattern, side, side), F32),
        in_specs=[pl.BlockSpec(memory_space=pltpu.HBM)] * len(operands),
        out_specs=pl.BlockSpec(memory_space=pltpu.VMEM),
        scratch_shapes=[
            *[pltpu.VMEM((vel_rows * inv_slots, side, side), F32)] * CLASS,
            pltpu.VMEM((listed, side, side), F32),
            pltpu.VMEM((2 * listed, side, side), F32),
            pltpu.VMEM((listed, side, side), F32),
            pltpu.VMEM((2 * listed, side, side), F32),
            pltpu.VMEM((listed, side, side), F32),
            pltpu.VMEM((2 * CLASS, 3, rows * side, 2 * vel_rows * side), BF16),
            pltpu.VMEM((CLASS, 3, vel_rows * side, 2 * vel_rows * side), BF16),
            pltpu.VMEM((2, rows, side, width), F32),
            pltpu.VMEM((rows, side, width), F32),
            pltpu.SMEM((1, META_WIDTH), jnp.int32),
            pltpu.SMEM((CLASS + 6, META_WIDTH), jnp.int32),
            *[pltpu.SMEM(value.shape, jnp.int32) for value in ints],
            pltpu.SemaphoreType.DMA((9,)),
            pltpu.SemaphoreType.DMA((9,)),
            pltpu.SemaphoreType.DMA((9,)),
            pltpu.SemaphoreType.DMA((12,)),
            pltpu.SemaphoreType.DMA((12,)),
            pltpu.SemaphoreType.DMA((18,)),
            pltpu.SemaphoreType.DMA((18,)),
            pltpu.SemaphoreType.DMA((rows,)),
            pltpu.SemaphoreType.DMA((rows,)),
        ],
        compiler_params=pltpu.CompilerParams(
            collective_id=0, has_side_effects=True, vmem_limit_bytes=56 * 2**20
        ),
    )(*operands)


def solution(mesh):
    placed = (
        P(("row", "col"), None, None, None),
        P(("row", "col"), None),
        P(("row", "col"), None),
        P(("row", "col")),
        P(("row", "col"), None, None, None),
        P(("row", "col"), None),
        P(("row", "col")),
        P(("row", "col"), None),
        P(("row", "col")),
    )
    return jax.shard_map(
        functools.partial(local, mesh.shape["col"]),
        mesh=mesh,
        in_specs=placed,
        out_specs=P(("row", "col"), None, None, None),
        check_vma=False,
    )
```

```python
import functools

import jax
import jax.numpy as jnp
from jax import lax
from jax.experimental import pallas as pl
from jax.experimental.pallas import tpu as pltpu
from jax.sharding import PartitionSpec as P

MESH = pl.DeviceIdType.MESH
F32 = jnp.float32
BF16 = jnp.bfloat16
SIDE = 4
CLASS = 8
META_WIDTH = 128


def halves(value):
    high = value.astype(BF16)
    return high, (value - high.astype(F32)).astype(BF16)


def kernel(
    lon_count,
    owner_hbm,
    local_hbm,
    count_hbm,
    cols_hbm,
    inv_count_hbm,
    pattern_hbm,
    pattern_count_hbm,
    div_ref,
    inv_ref,
    out_ref,
    *scratch,
):
    held = scratch[:CLASS]
    (
        div_own,
        div_own_side,
        div_mate,
        div_mate_side,
        div_pass,
        dense_div,
        dense_inv,
        sums,
        given,
        packet,
        meta,
        owner_ref,
        local_ref,
        count_ref,
        cols_ref,
        inv_count_ref,
        pattern_ref,
        pattern_count_ref,
        local_sem,
        div_send,
        div_recv,
        meta_send,
        meta_recv,
        inv_send,
        inv_recv,
        sum_send,
        sum_recv,
    ) = scratch[CLASS:]
    rows, slots_row = owner_ref.shape
    vel_rows, inv_slots = cols_ref.shape
    pattern = pattern_ref.shape[1]
    listed = rows * slots_row
    columns = 3 * vel_rows
    side = out_ref.shape[2]
    width = vel_rows * side
    row = lax.axis_index("row")
    col = lax.axis_index("col")
    odd = col % 2
    nxt = (col + 1) % lon_count
    prv = (col + lon_count - 1) % lon_count
    step_u = 1 + (SIDE - 1) * odd
    step_w = SIDE - (SIDE - 1) * odd
    u = (row // step_u) % SIDE
    w = (row // step_w) % SIDE

    def at(u_at, w_at):
        return u_at * step_u + w_at * step_w

    turn = 1 - 2 * (w % 2)

    def ring(amount):
        return (w + turn * amount + 2 * SIDE) % SIDE

    mate_row = at(u + 1 - 2 * (u % 2), w)
    other_row = at(u, w + 1 - 2 * (w % 2))
    across = at(SIDE - 1 - u, w)

    small = [
        pltpu.make_async_copy(src, dst, local_sem.at[i])
        for i, (src, dst) in enumerate(
            (
                (owner_hbm, owner_ref),
                (local_hbm, local_ref),
                (count_hbm, count_ref),
                (cols_hbm, cols_ref),
                (inv_count_hbm, inv_count_ref),
                (pattern_hbm, pattern_ref),
                (pattern_count_hbm, pattern_count_ref),
            )
        )
    ]
    for copy in small:
        copy.start()
    own_inv = pltpu.make_async_copy(inv_ref, held[0], local_sem.at[7])
    own_div = pltpu.make_async_copy(div_ref, div_own, local_sem.at[8])
    own_inv.start()
    own_div.start()

    kin = [(at(u, ring(k)), col) for k in (1, 2, 3)]
    kin += [(at(SIDE - 1 - u, ring(k)), col) for k in (0, 1, 2, 3)]
    near = [(mate_row, col), (row, nxt), (row, prv), (other_row, nxt), (other_row, prv)]
    heard = [(mate_row, nxt), (mate_row, prv)]
    barrier = pltpu.get_barrier_semaphore()
    for peer in kin + near + heard:
        pl.semaphore_signal(barrier, inc=1, device_id=peer, device_id_type=MESH)

    for copy in small:
        copy.wait()
    inv_at = listed
    pattern_at = inv_at + vel_rows * columns
    own_key = CLASS

    def note(place, value):
        packet[0, place] = value
        meta[0, place] = value
        meta[own_key, place] = value

    for slot in range(listed):
        p, k = slot // slots_row, slot % slots_row
        note(slot, jnp.where(k < count_ref[p], owner_ref[p, k] * vel_rows + local_ref[p, k], -1))
    for v in range(vel_rows):
        for column in range(columns):
            found = jnp.int32(-1)
            for m in range(inv_slots):
                hit = (cols_ref[v, m] == column) & (m < inv_count_ref[v])
                found = jnp.where(hit, m, found)
            note(inv_at + v * columns + column, found)
    for p in range(rows):
        for t in range(pattern):
            note(pattern_at + p * pattern + t, pattern_ref[p, t] % rows)

    pl.semaphore_wait(barrier, len(kin + near + heard))

    def remote(src, dst, send, recv, target):
        return pltpu.make_async_remote_copy(
            src_ref=src,
            dst_ref=dst,
            send_sem=send,
            recv_sem=recv,
            device_id=target,
            device_id_type=MESH,
        )

    def piece(offset, b, v, first, length):
        return held[(offset % SIDE) * 2 + b].at[pl.ds(v * inv_slots + first, length)]

    made = []

    def exchange(outgoing, placed, target):
        index = len(made)
        copy = remote(outgoing, placed, inv_send.at[index], inv_recv.at[index], (target, col))
        made.append(copy)
        return copy

    def own_piece(v):
        return inv_ref.at[pl.ds(v * inv_slots, inv_slots)]

    def ring_copies(v, b, source, cut):
        copies = []
        for way in (1, -1):
            copies.append(
                exchange(source, piece(way, b, v, 0, inv_slots), at(u, ring(way)))
            )
        for way, first, length in ((1, 0, cut), (-1, cut, inv_slots - cut)):
            copies.append(
                exchange(
                    piece(-way, b, v, first, length),
                    piece(2, b, v, first, length),
                    at(u, ring(way)),
                )
            )
        return copies

    def cross_copy(v, offset, first, length):
        outgoing = own_piece(v) if offset == 0 else piece(offset, 0, v, first, length)
        return exchange(outgoing, piece(offset, 1, v, first, length), across)

    cut = (inv_slots + 1) // 2
    cross_first = cross_copy(0, 0, 0, inv_slots)
    ring_own = ring_copies(0, 0, own_piece(0), cut)
    ring_far = ring_copies(0, 1, piece(0, 1, 0, 0, inv_slots), inv_slots - cut)
    ring_last = ring_copies(1, 0, own_piece(1), cut)
    cross_last = [
        cross_copy(1, 0, 0, inv_slots),
        cross_copy(1, -1, 0, inv_slots),
        cross_copy(1, 1, 0, inv_slots),
        cross_copy(1, 2, 0, cut),
        cross_copy(1, 2, cut, inv_slots - cut),
    ]

    plan = []
    for part in range(2):
        some = pl.ds(part * slots_row, slots_row)
        plan.append((div_ref.at[some], div_pass.at[some], (other_row, col)))
    plan += [
        (div_ref, div_own_side.at[pl.ds(0, listed)], (row, nxt)),
        (div_ref, div_own_side.at[pl.ds(listed, listed)], (row, prv)),
        (div_ref, div_mate, (mate_row, col)),
    ]
    for part in range(2):
        some = pl.ds(part * slots_row, slots_row)
        for third, target in ((1, nxt), (2, prv)):
            there = pl.ds((third - 1) * listed + part * slots_row, slots_row)
            plan.append((div_pass.at[some], div_mate_side.at[there], (row, target)))
    div_copies = [
        remote(src, dst, div_send.at[i], div_recv.at[i], peer)
        for i, (src, dst, peer) in enumerate(plan)
    ]

    meta_rows = [k * 2 for k in (1, 2, 3)]
    meta_rows += [k * 2 + 1 for k in (0, 1, 2, 3)]
    meta_rows += [own_key + 3, own_key + 1, own_key + 2, own_key + 4, own_key + 5]
    meta_copies = [
        remote(packet, meta.at[pl.ds(meta_rows[i], 1)], meta_send.at[i], meta_recv.at[i], peer)
        for i, peer in enumerate(kin + near)
    ]

    def spread(group, thirds):
        keys_own = own_key + 3 * group
        home, beside = ((div_own, div_own_side), (div_mate, div_mate_side))[group]

        def one(rel, carry):
            owner_u = u + (rel % 2) * (SIDE - 1 - 2 * u)
            owner = at(owner_u, ring(rel // 2))
            for third in thirds:
                for p in range(rows):
                    base = p * slots_row
                    if third:
                        t = 3 if third == 1 else 2
                        base = meta[keys_own, pattern_at + p * pattern + t] * slots_row
                    for c in range(vel_rows):
                        wanted = owner * vel_rows + c
                        first, second = jnp.int32(-1), jnp.int32(-1)
                        for l in range(slots_row):
                            hit = meta[keys_own + third, base + l] == wanted
                            second = jnp.where(hit, first, second)
                            first = jnp.where(hit, l, first)
                        one_on = jnp.where(first >= 0, 1.0, 0.0)
                        two_on = jnp.where(second >= 0, 1.0, 0.0)
                        source = beside if third else home
                        here = max(third - 1, 0) * listed + base
                        value = (
                            one_on * source[here + jnp.maximum(first, 0)]
                            + two_on * source[here + jnp.maximum(second, 0)]
                        )
                        high, low = halves(value)
                        place = group * CLASS + rel
                        lines = slice(p * side, (p + 1) * side)
                        at_high = slice(c * side, (c + 1) * side)
                        at_low = slice(width + c * side, width + (c + 1) * side)
                        dense_div[place, third, lines, at_high] = high
                        dense_div[place, third, lines, at_low] = low
            return carry

        lax.fori_loop(0, CLASS, one, 0)

    def gather(rel):
        for v in range(vel_rows):
            for column in range(columns):
                place = meta[rel, inv_at + v * columns + column]
                on = jnp.where(place >= 0, 1.0, 0.0)
                high, low = halves(on * held[rel][v * inv_slots + jnp.maximum(place, 0)])
                third = (1, 0, 2)[column // vel_rows]
                c = column % vel_rows
                lines = slice(v * side, (v + 1) * side)
                dense_inv[rel, third, lines, c * side : (c + 1) * side] = high
                dense_inv[rel, third, lines, width + c * side : width + (c + 1) * side] = low

    def product(rel, group, only=None):
        place = group * CLASS + rel
        factors = []
        for third in range(3):
            inv = dense_inv[rel, third]
            div = dense_div[place, third]
            inv_high, inv_low = inv[:, :width], inv[:, width:]
            div_high, div_low = div[:, :width], div[:, width:]
            value = lax.dot_general(
                jnp.concatenate([inv_high, inv_high, inv_low], axis=1),
                jnp.concatenate([div_high, div_low, div_high], axis=1),
                (((1,), (1,)), ((), ())),
                preferred_element_type=F32,
            )
            factors.append(halves(value))
        for p in range(rows):
            order = ((0, p), (0, 1 - p), (2, p), (1, p))
            high, low = (
                jnp.concatenate(
                    [factors[third][i][:, q * side : (q + 1) * side] for third, q in order], axis=1
                )
                for i in range(2)
            )
            left = dense_div[place, 0, p * side : (p + 1) * side, :]
            left_high, left_low = left[:, :width], left[:, width:]
            sums[group, p] += jnp.dot(
                jnp.concatenate([left_high, left_high, left_low], axis=1),
                jnp.concatenate([high, low, high], axis=0),
                preferred_element_type=F32,
            )
            if only is not None:
                only[p].start()

    cross_first.start()
    ring_last[0].start()
    ring_last[1].start()
    ring_own[0].start()
    ring_own[1].start()
    cross_last[0].start()
    div_copies[4].start()
    div_copies[2].start()
    div_copies[3].start()
    div_copies[0].start()
    div_copies[1].start()
    for copy in meta_copies:
        copy.start()
    sums[...] = jnp.zeros_like(sums)
    own_inv.wait()
    own_div.wait()
    cross_first.wait_recv()
    ring_far[0].start()
    ring_far[1].start()
    ring_last[0].wait_recv()
    ring_last[3].start()
    cross_last[2].start()
    ring_last[1].wait_recv()
    ring_last[2].start()
    cross_last[1].start()
    spread(0, (0,))
    ring_own[0].wait_recv()
    ring_own[3].start()
    ring_own[1].wait_recv()
    ring_own[2].start()
    div_copies[0].wait_recv()
    div_copies[5].start()
    div_copies[6].start()
    div_copies[1].wait_recv()
    div_copies[7].start()
    div_copies[8].start()
    ring_last[2].wait_recv()
    cross_last[3].start()
    ring_last[3].wait_recv()
    cross_last[4].start()
    ring_far[0].wait_recv()
    ring_far[3].start()
    ring_far[1].wait_recv()
    ring_far[2].start()
    for copy in meta_copies:
        copy.wait_recv()
    div_copies[2].wait_recv()
    div_copies[3].wait_recv()
    spread(0, (1,2,))
    gather(0)
    product(0, 0)
    cross_last[0].wait_recv()
    gather(1)
    product(1, 0)
    gather(2)
    product(2, 0)
    gather(6)
    product(6, 0)
    div_copies[4].wait_recv()
    spread(1, (0,))
    ring_own[2].wait_recv()
    ring_own[3].wait_recv()
    gather(4)
    product(4, 0)
    div_copies[5].wait_recv()
    div_copies[6].wait_recv()
    div_copies[7].wait_recv()
    div_copies[8].wait_recv()
    spread(1, (1,2,))
    product(0, 1)
    product(1, 1)
    product(2, 1)
    product(6, 1)
    product(4, 1)
    cross_last[2].wait_recv()
    gather(3)
    product(3, 0)
    product(3, 1)
    cross_last[1].wait_recv()
    gather(7)
    product(7, 0)
    product(7, 1)
    cross_last[3].wait_recv()
    cross_last[4].wait_recv()
    ring_far[2].wait_recv()
    ring_far[3].wait_recv()
    gather(5)
    returns = [
        remote(
            sums.at[1, pl.ds(p, 1)],
            given.at[pl.ds(p, 1)],
            sum_send.at[p],
            sum_recv.at[p],
            (mate_row, col),
        )
        for p in range(rows)
    ]
    product(5, 1, returns)
    product(5, 0)
    for p in range(rows):
        returns[p].wait_recv()
        total = sums[0, p] + given[p]
        for t in range(pattern):
            kept = jnp.where(t < pattern_count_ref[p], 1.0, 0.0)
            out_ref[p, t] = kept * total[:, t * side : (t + 1) * side]

    for copy in (*meta_copies, *div_copies, *made, *returns):
        copy.wait_send()


def local(
    lon_count,
    div_blocks,
    div_owner,
    div_local,
    div_count,
    inv_blocks,
    inv_cols,
    inv_count,
    schur_cols,
    schur_count,
):
    rows, slots_row, side, _ = div_blocks.shape
    vel_rows, inv_slots = inv_cols.shape
    pattern = schur_cols.shape[1]
    listed = rows * slots_row
    width = pattern * side
    ints = (div_owner, div_local, div_count, inv_cols, inv_count, schur_cols, schur_count)
    operands = [
        pltpu.with_memory_space_constraint(value, pltpu.HBM)
        for value in (
            *ints,
            div_blocks.reshape(listed, side, side),
            inv_blocks.reshape(vel_rows * inv_slots, side, side),
        )
    ]
    return pl.pallas_call(
        functools.partial(kernel, lon_count),
        out_shape=jax.ShapeDtypeStruct((rows, pattern, side, side), F32),
        in_specs=[pl.BlockSpec(memory_space=pltpu.HBM)] * len(operands),
        out_specs=pl.BlockSpec(memory_space=pltpu.VMEM),
        scratch_shapes=[
            *[pltpu.VMEM((vel_rows * inv_slots, side, side), F32)] * CLASS,
            pltpu.VMEM((listed, side, side), F32),
            pltpu.VMEM((2 * listed, side, side), F32),
            pltpu.VMEM((listed, side, side), F32),
            pltpu.VMEM((2 * listed, side, side), F32),
            pltpu.VMEM((listed, side, side), F32),
            pltpu.VMEM((2 * CLASS, 3, rows * side, 2 * vel_rows * side), BF16),
            pltpu.VMEM((CLASS, 3, vel_rows * side, 2 * vel_rows * side), BF16),
            pltpu.VMEM((2, rows, side, width), F32),
            pltpu.VMEM((rows, side, width), F32),
            pltpu.SMEM((1, META_WIDTH), jnp.int32),
            pltpu.SMEM((CLASS + 6, META_WIDTH), jnp.int32),
            *[pltpu.SMEM(value.shape, jnp.int32) for value in ints],
            pltpu.SemaphoreType.DMA((9,)),
            pltpu.SemaphoreType.DMA((9,)),
            pltpu.SemaphoreType.DMA((9,)),
            pltpu.SemaphoreType.DMA((12,)),
            pltpu.SemaphoreType.DMA((12,)),
            pltpu.SemaphoreType.DMA((18,)),
            pltpu.SemaphoreType.DMA((18,)),
            pltpu.SemaphoreType.DMA((rows,)),
            pltpu.SemaphoreType.DMA((rows,)),
        ],
        compiler_params=pltpu.CompilerParams(
            collective_id=0, has_side_effects=True, vmem_limit_bytes=56 * 2**20
        ),
    )(*operands)


def solution(mesh):
    placed = (
        P(("row", "col"), None, None, None),
        P(("row", "col"), None),
        P(("row", "col"), None),
        P(("row", "col")),
        P(("row", "col"), None, None, None),
        P(("row", "col"), None),
        P(("row", "col")),
        P(("row", "col"), None),
        P(("row", "col")),
    )
    return jax.shard_map(
        functools.partial(local, mesh.shape["col"]),
        mesh=mesh,
        in_specs=placed,
        out_specs=P(("row", "col"), None, None, None),
        check_vma=False,
    )
```

```python
import functools

import jax
import jax.numpy as jnp
from jax import lax
from jax.experimental import pallas as pl
from jax.experimental.pallas import tpu as pltpu
from jax.sharding import PartitionSpec as P

MESH = pl.DeviceIdType.MESH
F32 = jnp.float32
BF16 = jnp.bfloat16
SIDE = 4
CLASS = 8
META_WIDTH = 128


def halves(value):
    high = value.astype(BF16)
    return high, (value - high.astype(F32)).astype(BF16)


def kernel(
    lon_count,
    owner_hbm,
    local_hbm,
    count_hbm,
    cols_hbm,
    inv_count_hbm,
    pattern_hbm,
    pattern_count_hbm,
    div_ref,
    inv_ref,
    out_ref,
    *scratch,
):
    held = scratch[:CLASS]
    (
        div_own,
        div_own_side,
        div_mate,
        div_mate_side,
        div_pass,
        dense_div,
        dense_inv,
        sums,
        given,
        packet,
        meta,
        picks,
        owner_ref,
        local_ref,
        count_ref,
        cols_ref,
        inv_count_ref,
        pattern_ref,
        pattern_count_ref,
        local_sem,
        div_send,
        div_recv,
        meta_send,
        meta_recv,
        inv_send,
        inv_recv,
        sum_send,
        sum_recv,
    ) = scratch[CLASS:]
    rows, slots_row = owner_ref.shape
    vel_rows, inv_slots = cols_ref.shape
    pattern = pattern_ref.shape[1]
    listed = rows * slots_row
    columns = 3 * vel_rows
    side = out_ref.shape[2]
    width = vel_rows * side
    row = lax.axis_index("row")
    col = lax.axis_index("col")
    odd = col % 2
    nxt = (col + 1) % lon_count
    prv = (col + lon_count - 1) % lon_count
    step_u = 1 + (SIDE - 1) * odd
    step_w = SIDE - (SIDE - 1) * odd
    u = (row // step_u) % SIDE
    w = (row // step_w) % SIDE

    def at(u_at, w_at):
        return u_at * step_u + w_at * step_w

    turn = 1 - 2 * (w % 2)

    def ring(amount):
        return (w + turn * amount + 2 * SIDE) % SIDE

    mate_row = at(u + 1 - 2 * (u % 2), w)
    other_row = at(u, w + 1 - 2 * (w % 2))
    across = at(SIDE - 1 - u, w)

    small = [
        pltpu.make_async_copy(src, dst, local_sem.at[i])
        for i, (src, dst) in enumerate(
            (
                (owner_hbm, owner_ref),
                (local_hbm, local_ref),
                (count_hbm, count_ref),
                (cols_hbm, cols_ref),
                (inv_count_hbm, inv_count_ref),
                (pattern_hbm, pattern_ref),
                (pattern_count_hbm, pattern_count_ref),
            )
        )
    ]
    for copy in small:
        copy.start()
    own_inv = pltpu.make_async_copy(inv_ref, held[0], local_sem.at[7])
    own_div = pltpu.make_async_copy(div_ref, div_own, local_sem.at[8])
    own_inv.start()
    own_div.start()

    kin = [(at(u, ring(k)), col) for k in (1, 2, 3)]
    kin += [(at(SIDE - 1 - u, ring(k)), col) for k in (0, 1, 2, 3)]
    near = [(mate_row, col), (row, nxt), (row, prv), (other_row, nxt), (other_row, prv)]
    heard = [(mate_row, nxt), (mate_row, prv)]
    barrier = pltpu.get_barrier_semaphore()
    for peer in kin + near + heard:
        pl.semaphore_signal(barrier, inc=1, device_id=peer, device_id_type=MESH)

    for copy in small:
        copy.wait()
    inv_at = listed
    pattern_at = inv_at + vel_rows * columns
    own_key = CLASS

    def note(place, value):
        packet[0, place] = value
        meta[0, place] = value
        meta[own_key, place] = value

    for slot in range(listed):
        p, k = slot // slots_row, slot % slots_row
        note(slot, jnp.where(k < count_ref[p], owner_ref[p, k] * vel_rows + local_ref[p, k], -1))
    for v in range(vel_rows):
        for column in range(columns):
            found = jnp.int32(-1)
            for m in range(inv_slots):
                hit = (cols_ref[v, m] == column) & (m < inv_count_ref[v])
                found = jnp.where(hit, m, found)
            note(inv_at + v * columns + column, found)
    for p in range(rows):
        for t in range(pattern):
            note(pattern_at + p * pattern + t, pattern_ref[p, t] % rows)

    pl.semaphore_wait(barrier, len(kin + near + heard))

    def remote(src, dst, send, recv, target):
        return pltpu.make_async_remote_copy(
            src_ref=src,
            dst_ref=dst,
            send_sem=send,
            recv_sem=recv,
            device_id=target,
            device_id_type=MESH,
        )

    def piece(offset, b, v, first, length):
        return held[(offset % SIDE) * 2 + b].at[pl.ds(v * inv_slots + first, length)]

    made = []

    def exchange(outgoing, placed, target):
        index = len(made)
        copy = remote(outgoing, placed, inv_send.at[index], inv_recv.at[index], (target, col))
        made.append(copy)
        return copy

    def own_piece(v):
        return inv_ref.at[pl.ds(v * inv_slots, inv_slots)]

    def ring_copies(v, b, source, cut):
        copies = []
        for way in (1, -1):
            copies.append(
                exchange(source, piece(way, b, v, 0, inv_slots), at(u, ring(way)))
            )
        for way, first, length in ((1, 0, cut), (-1, cut, inv_slots - cut)):
            copies.append(
                exchange(
                    piece(-way, b, v, first, length),
                    piece(2, b, v, first, length),
                    at(u, ring(way)),
                )
            )
        return copies

    def cross_copy(v, offset, first, length):
        outgoing = own_piece(v) if offset == 0 else piece(offset, 0, v, first, length)
        return exchange(outgoing, piece(offset, 1, v, first, length), across)

    cut = (inv_slots + 1) // 2
    cross_first = cross_copy(0, 0, 0, inv_slots)
    ring_own = ring_copies(0, 0, own_piece(0), cut)
    ring_far = ring_copies(0, 1, piece(0, 1, 0, 0, inv_slots), inv_slots - cut)
    ring_last = ring_copies(1, 0, own_piece(1), cut)
    cross_last = [
        cross_copy(1, 0, 0, inv_slots),
        cross_copy(1, -1, 0, inv_slots),
        cross_copy(1, 1, 0, inv_slots),
        cross_copy(1, 2, 0, cut),
        cross_copy(1, 2, cut, inv_slots - cut),
    ]

    plan = []
    for part in range(2):
        some = pl.ds(part * slots_row, slots_row)
        plan.append((div_ref.at[some], div_pass.at[some], (other_row, col)))
    plan += [
        (div_ref, div_own_side.at[pl.ds(0, listed)], (row, nxt)),
        (div_ref, div_own_side.at[pl.ds(listed, listed)], (row, prv)),
        (div_ref, div_mate, (mate_row, col)),
    ]
    for part in range(2):
        some = pl.ds(part * slots_row, slots_row)
        for third, target in ((1, nxt), (2, prv)):
            there = pl.ds((third - 1) * listed + part * slots_row, slots_row)
            plan.append((div_pass.at[some], div_mate_side.at[there], (row, target)))
    div_copies = [
        remote(src, dst, div_send.at[i], div_recv.at[i], peer)
        for i, (src, dst, peer) in enumerate(plan)
    ]

    meta_rows = [k * 2 for k in (1, 2, 3)]
    meta_rows += [k * 2 + 1 for k in (0, 1, 2, 3)]
    meta_rows += [own_key + 3, own_key + 1, own_key + 2, own_key + 4, own_key + 5]
    meta_copies = [
        remote(packet, meta.at[pl.ds(meta_rows[i], 1)], meta_send.at[i], meta_recv.at[i], peer)
        for i, peer in enumerate(kin + near)
    ]

    def find(group):
        keys_own = own_key + 3 * group

        def one(rel, carry):
            owner_u = u + (rel % 2) * (SIDE - 1 - 2 * u)
            owner = at(owner_u, ring(rel // 2))
            for third in range(3):
                for p in range(rows):
                    base = p * slots_row
                    if third:
                        t = 3 if third == 1 else 2
                        base = meta[keys_own, pattern_at + p * pattern + t] * slots_row
                    for c in range(vel_rows):
                        wanted = owner * vel_rows + c
                        first, second = jnp.int32(-1), jnp.int32(-1)
                        for l in range(slots_row):
                            hit = meta[keys_own + third, base + l] == wanted
                            second = jnp.where(hit, first, second)
                            first = jnp.where(hit, max(third - 1, 0) * listed + base + l, first)
                        entry = ((third * rows + p) * vel_rows + c) * 2
                        picks[group * CLASS + rel, entry] = first
                        picks[group * CLASS + rel, entry + 1] = second
            return carry

        lax.fori_loop(0, CLASS, one, 0)

    def spread(group, thirds):
        home, beside = ((div_own, div_own_side), (div_mate, div_mate_side))[group]

        def one(rel, carry):
            place = group * CLASS + rel
            for third in thirds:
                source = beside if third else home
                for p in range(rows):
                    for c in range(vel_rows):
                        entry = ((third * rows + p) * vel_rows + c) * 2
                        first, second = picks[place, entry], picks[place, entry + 1]
                        one_on = jnp.where(first >= 0, 1.0, 0.0)
                        two_on = jnp.where(second >= 0, 1.0, 0.0)
                        value = (
                            one_on * source[jnp.maximum(first, 0)]
                            + two_on * source[jnp.maximum(second, 0)]
                        )
                        high, low = halves(value)
                        lines = slice(p * side, (p + 1) * side)
                        at_high = slice(c * side, (c + 1) * side)
                        at_low = slice(width + c * side, width + (c + 1) * side)
                        dense_div[place, third, lines, at_high] = high
                        dense_div[place, third, lines, at_low] = low
            return carry

        lax.fori_loop(0, CLASS, one, 0)

    def gather(rel):
        for v in range(vel_rows):
            for column in range(columns):
                place = meta[rel, inv_at + v * columns + column]
                on = jnp.where(place >= 0, 1.0, 0.0)
                high, low = halves(on * held[rel][v * inv_slots + jnp.maximum(place, 0)])
                third = (1, 0, 2)[column // vel_rows]
                c = column % vel_rows
                lines = slice(v * side, (v + 1) * side)
                dense_inv[rel, third, lines, c * side : (c + 1) * side] = high
                dense_inv[rel, third, lines, width + c * side : width + (c + 1) * side] = low

    def product(rel, group, only=None):
        place = group * CLASS + rel
        factors = []
        for third in range(3):
            inv = dense_inv[rel, third]
            div = dense_div[place, third]
            inv_high, inv_low = inv[:, :width], inv[:, width:]
            div_high, div_low = div[:, :width], div[:, width:]
            value = lax.dot_general(
                jnp.concatenate([inv_high, inv_high, inv_low], axis=1),
                jnp.concatenate([div_high, div_low, div_high], axis=1),
                (((1,), (1,)), ((), ())),
                preferred_element_type=F32,
            )
            factors.append(halves(value))
        for p in range(rows):
            order = ((0, p), (0, 1 - p), (2, p), (1, p))
            high, low = (
                jnp.concatenate(
                    [factors[third][i][:, q * side : (q + 1) * side] for third, q in order], axis=1
                )
                for i in range(2)
            )
            left = dense_div[place, 0, p * side : (p + 1) * side, :]
            left_high, left_low = left[:, :width], left[:, width:]
            sums[group, p] += jnp.dot(
                jnp.concatenate([left_high, left_high, left_low], axis=1),
                jnp.concatenate([high, low, high], axis=0),
                preferred_element_type=F32,
            )
            if only is not None:
                only[p].start()

    for copy in meta_copies:
        copy.start()
    cross_first.start()
    ring_last[0].start()
    ring_last[1].start()
    ring_own[0].start()
    ring_own[1].start()
    cross_last[0].start()
    div_copies[0].start()
    div_copies[1].start()
    div_copies[2].start()
    div_copies[3].start()
    div_copies[4].start()
    sums[...] = jnp.zeros_like(sums)
    own_inv.wait()
    own_div.wait()
    cross_first.wait_recv()
    ring_far[0].start()
    ring_far[1].start()
    ring_last[0].wait_recv()
    ring_last[3].start()
    cross_last[2].start()
    ring_last[1].wait_recv()
    ring_last[2].start()
    cross_last[1].start()
    for copy in meta_copies:
        copy.wait_recv()
    find(0)
    div_copies[0].wait_recv()
    div_copies[5].start()
    div_copies[6].start()
    ring_own[0].wait_recv()
    ring_own[3].start()
    ring_own[1].wait_recv()
    ring_own[2].start()
    div_copies[1].wait_recv()
    div_copies[7].start()
    div_copies[8].start()
    find(1)
    spread(0, (0,))
    ring_last[2].wait_recv()
    cross_last[3].start()
    ring_last[3].wait_recv()
    cross_last[4].start()
    div_copies[2].wait_recv()
    div_copies[3].wait_recv()
    spread(0, (1,2,))
    gather(0)
    product(0, 0)
    ring_far[0].wait_recv()
    ring_far[3].start()
    ring_far[1].wait_recv()
    ring_far[2].start()
    cross_last[0].wait_recv()
    gather(1)
    product(1, 0)
    gather(2)
    product(2, 0)
    gather(6)
    product(6, 0)
    div_copies[4].wait_recv()
    spread(1, (0,))
    ring_own[2].wait_recv()
    ring_own[3].wait_recv()
    gather(4)
    product(4, 0)
    div_copies[5].wait_recv()
    div_copies[6].wait_recv()
    div_copies[7].wait_recv()
    div_copies[8].wait_recv()
    spread(1, (1,2,))
    product(0, 1)
    product(1, 1)
    product(2, 1)
    product(6, 1)
    product(4, 1)
    cross_last[2].wait_recv()
    gather(3)
    product(3, 1)
    cross_last[1].wait_recv()
    gather(7)
    product(7, 1)
    cross_last[3].wait_recv()
    cross_last[4].wait_recv()
    ring_far[2].wait_recv()
    ring_far[3].wait_recv()
    gather(5)
    returns = [
        remote(
            sums.at[1, pl.ds(p, 1)],
            given.at[pl.ds(p, 1)],
            sum_send.at[p],
            sum_recv.at[p],
            (mate_row, col),
        )
        for p in range(rows)
    ]
    product(5, 1, returns)
    product(3, 0)
    product(7, 0)
    product(5, 0)
    for p in range(rows):
        returns[p].wait_recv()
        total = sums[0, p] + given[p]
        for t in range(pattern):
            kept = jnp.where(t < pattern_count_ref[p], 1.0, 0.0)
            out_ref[p, t] = kept * total[:, t * side : (t + 1) * side]

    for copy in (*meta_copies, *div_copies, *made, *returns):
        copy.wait_send()


def local(
    lon_count,
    div_blocks,
    div_owner,
    div_local,
    div_count,
    inv_blocks,
    inv_cols,
    inv_count,
    schur_cols,
    schur_count,
):
    rows, slots_row, side, _ = div_blocks.shape
    vel_rows, inv_slots = inv_cols.shape
    pattern = schur_cols.shape[1]
    listed = rows * slots_row
    width = pattern * side
    ints = (div_owner, div_local, div_count, inv_cols, inv_count, schur_cols, schur_count)
    operands = [
        pltpu.with_memory_space_constraint(value, pltpu.HBM)
        for value in (
            *ints,
            div_blocks.reshape(listed, side, side),
            inv_blocks.reshape(vel_rows * inv_slots, side, side),
        )
    ]
    return pl.pallas_call(
        functools.partial(kernel, lon_count),
        out_shape=jax.ShapeDtypeStruct((rows, pattern, side, side), F32),
        in_specs=[pl.BlockSpec(memory_space=pltpu.HBM)] * len(operands),
        out_specs=pl.BlockSpec(memory_space=pltpu.VMEM),
        scratch_shapes=[
            *[pltpu.VMEM((vel_rows * inv_slots, side, side), F32)] * CLASS,
            pltpu.VMEM((listed, side, side), F32),
            pltpu.VMEM((2 * listed, side, side), F32),
            pltpu.VMEM((listed, side, side), F32),
            pltpu.VMEM((2 * listed, side, side), F32),
            pltpu.VMEM((listed, side, side), F32),
            pltpu.VMEM((2 * CLASS, 3, rows * side, 2 * vel_rows * side), BF16),
            pltpu.VMEM((CLASS, 3, vel_rows * side, 2 * vel_rows * side), BF16),
            pltpu.VMEM((2, rows, side, width), F32),
            pltpu.VMEM((rows, side, width), F32),
            pltpu.SMEM((1, META_WIDTH), jnp.int32),
            pltpu.SMEM((CLASS + 6, META_WIDTH), jnp.int32),
            pltpu.SMEM((2 * CLASS, 6 * rows * vel_rows), jnp.int32),
            *[pltpu.SMEM(value.shape, jnp.int32) for value in ints],
            pltpu.SemaphoreType.DMA((9,)),
            pltpu.SemaphoreType.DMA((9,)),
            pltpu.SemaphoreType.DMA((9,)),
            pltpu.SemaphoreType.DMA((12,)),
            pltpu.SemaphoreType.DMA((12,)),
            pltpu.SemaphoreType.DMA((18,)),
            pltpu.SemaphoreType.DMA((18,)),
            pltpu.SemaphoreType.DMA((rows,)),
            pltpu.SemaphoreType.DMA((rows,)),
        ],
        compiler_params=pltpu.CompilerParams(
            collective_id=0, has_side_effects=True, vmem_limit_bytes=56 * 2**20
        ),
    )(*operands)


def solution(mesh):
    placed = (
        P(("row", "col"), None, None, None),
        P(("row", "col"), None),
        P(("row", "col"), None),
        P(("row", "col")),
        P(("row", "col"), None, None, None),
        P(("row", "col"), None),
        P(("row", "col")),
        P(("row", "col"), None),
        P(("row", "col")),
    )
    return jax.shard_map(
        functools.partial(local, mesh.shape["col"]),
        mesh=mesh,
        in_specs=placed,
        out_specs=P(("row", "col"), None, None, None),
        check_vma=False,
    )
```

```python
import functools

import jax
import jax.numpy as jnp
from jax import lax
from jax.experimental import pallas as pl
from jax.experimental.pallas import tpu as pltpu
from jax.sharding import PartitionSpec as P

MESH = pl.DeviceIdType.MESH
F32 = jnp.float32
BF16 = jnp.bfloat16
SIDE = 4
CLASS = 8
META_WIDTH = 128


def halves(value):
    high = value.astype(BF16)
    return high, (value - high.astype(F32)).astype(BF16)


def kernel(
    lon_count,
    owner_hbm,
    local_hbm,
    count_hbm,
    cols_hbm,
    inv_count_hbm,
    pattern_hbm,
    pattern_count_hbm,
    div_ref,
    inv_ref,
    out_ref,
    *scratch,
):
    held = scratch[:CLASS]
    (
        div_own,
        div_own_side,
        div_mate,
        div_mate_side,
        div_pass,
        dense_div,
        dense_inv,
        sums,
        given,
        packet,
        meta,
        picks,
        owner_ref,
        local_ref,
        count_ref,
        cols_ref,
        inv_count_ref,
        pattern_ref,
        pattern_count_ref,
        local_sem,
        div_send,
        div_recv,
        meta_send,
        meta_recv,
        inv_send,
        inv_recv,
        sum_send,
        sum_recv,
    ) = scratch[CLASS:]
    rows, slots_row = owner_ref.shape
    vel_rows, inv_slots = cols_ref.shape
    pattern = pattern_ref.shape[1]
    listed = rows * slots_row
    columns = 3 * vel_rows
    side = out_ref.shape[2]
    width = vel_rows * side
    row = lax.axis_index("row")
    col = lax.axis_index("col")
    odd = col % 2
    nxt = (col + 1) % lon_count
    prv = (col + lon_count - 1) % lon_count
    step_u = 1 + (SIDE - 1) * odd
    step_w = SIDE - (SIDE - 1) * odd
    u = (row // step_u) % SIDE
    w = (row // step_w) % SIDE

    def at(u_at, w_at):
        return u_at * step_u + w_at * step_w

    turn = 1 - 2 * (w % 2)

    def ring(amount):
        return (w + turn * amount + 2 * SIDE) % SIDE

    mate_row = at(u + 1 - 2 * (u % 2), w)
    other_row = at(u, w + 1 - 2 * (w % 2))
    across = at(SIDE - 1 - u, w)

    small = [
        pltpu.make_async_copy(src, dst, local_sem.at[i])
        for i, (src, dst) in enumerate(
            (
                (owner_hbm, owner_ref),
                (local_hbm, local_ref),
                (count_hbm, count_ref),
                (cols_hbm, cols_ref),
                (inv_count_hbm, inv_count_ref),
                (pattern_hbm, pattern_ref),
                (pattern_count_hbm, pattern_count_ref),
            )
        )
    ]
    for copy in small:
        copy.start()
    own_inv = pltpu.make_async_copy(inv_ref, held[0], local_sem.at[7])
    own_div = pltpu.make_async_copy(div_ref, div_own, local_sem.at[8])
    own_inv.start()
    own_div.start()

    kin = [(at(u, ring(k)), col) for k in (1, 2, 3)]
    kin += [(at(SIDE - 1 - u, ring(k)), col) for k in (0, 1, 2, 3)]
    near = [(mate_row, col), (row, nxt), (row, prv), (other_row, nxt), (other_row, prv)]
    heard = [(mate_row, nxt), (mate_row, prv)]
    barrier = pltpu.get_barrier_semaphore()
    for peer in kin + near + heard:
        pl.semaphore_signal(barrier, inc=1, device_id=peer, device_id_type=MESH)

    for copy in small:
        copy.wait()
    inv_at = listed
    pattern_at = inv_at + vel_rows * columns
    own_key = CLASS

    def note(place, value):
        packet[0, place] = value
        meta[0, place] = value
        meta[own_key, place] = value

    for slot in range(listed):
        p, k = slot // slots_row, slot % slots_row
        note(slot, jnp.where(k < count_ref[p], owner_ref[p, k] * vel_rows + local_ref[p, k], -1))
    for v in range(vel_rows):
        for column in range(columns):
            found = jnp.int32(-1)
            for m in range(inv_slots):
                hit = (cols_ref[v, m] == column) & (m < inv_count_ref[v])
                found = jnp.where(hit, m, found)
            note(inv_at + v * columns + column, found)
    for p in range(rows):
        for t in range(pattern):
            note(pattern_at + p * pattern + t, pattern_ref[p, t] % rows)

    pl.semaphore_wait(barrier, len(kin + near + heard))

    def remote(src, dst, send, recv, target):
        return pltpu.make_async_remote_copy(
            src_ref=src,
            dst_ref=dst,
            send_sem=send,
            recv_sem=recv,
            device_id=target,
            device_id_type=MESH,
        )

    def piece(offset, b, v, first, length):
        return held[(offset % SIDE) * 2 + b].at[pl.ds(v * inv_slots + first, length)]

    made = []

    def exchange(outgoing, placed, target):
        index = len(made)
        copy = remote(outgoing, placed, inv_send.at[index], inv_recv.at[index], (target, col))
        made.append(copy)
        return copy

    def own_piece(v):
        return inv_ref.at[pl.ds(v * inv_slots, inv_slots)]

    def ring_copies(v, b, source, cut):
        copies = []
        for way in (1, -1):
            copies.append(
                exchange(source, piece(way, b, v, 0, inv_slots), at(u, ring(way)))
            )
        for way, first, length in ((1, 0, cut), (-1, cut, inv_slots - cut)):
            copies.append(
                exchange(
                    piece(-way, b, v, first, length),
                    piece(2, b, v, first, length),
                    at(u, ring(way)),
                )
            )
        return copies

    def cross_copy(v, offset, first, length):
        outgoing = own_piece(v) if offset == 0 else piece(offset, 0, v, first, length)
        return exchange(outgoing, piece(offset, 1, v, first, length), across)

    cut = (inv_slots + 1) // 2
    cross_first = cross_copy(0, 0, 0, inv_slots)
    ring_own = ring_copies(0, 0, own_piece(0), cut)
    ring_far = ring_copies(0, 1, piece(0, 1, 0, 0, inv_slots), inv_slots - cut)
    ring_last = ring_copies(1, 0, own_piece(1), cut)
    cross_last = [
        cross_copy(1, 0, 0, inv_slots),
        cross_copy(1, -1, 0, inv_slots),
        cross_copy(1, 1, 0, inv_slots),
        cross_copy(1, 2, 0, cut),
        cross_copy(1, 2, cut, inv_slots - cut),
    ]

    plan = []
    for part in range(2):
        some = pl.ds(part * slots_row, slots_row)
        plan.append((div_ref.at[some], div_pass.at[some], (other_row, col)))
    plan += [
        (div_ref, div_own_side.at[pl.ds(0, listed)], (row, nxt)),
        (div_ref, div_own_side.at[pl.ds(listed, listed)], (row, prv)),
        (div_ref, div_mate, (mate_row, col)),
    ]
    for part in range(2):
        some = pl.ds(part * slots_row, slots_row)
        for third, target in ((1, nxt), (2, prv)):
            there = pl.ds((third - 1) * listed + part * slots_row, slots_row)
            plan.append((div_pass.at[some], div_mate_side.at[there], (row, target)))
    div_copies = [
        remote(src, dst, div_send.at[i], div_recv.at[i], peer)
        for i, (src, dst, peer) in enumerate(plan)
    ]

    meta_rows = [k * 2 for k in (1, 2, 3)]
    meta_rows += [k * 2 + 1 for k in (0, 1, 2, 3)]
    meta_rows += [own_key + 3, own_key + 1, own_key + 2, own_key + 4, own_key + 5]
    meta_copies = [
        remote(packet, meta.at[pl.ds(meta_rows[i], 1)], meta_send.at[i], meta_recv.at[i], peer)
        for i, peer in enumerate(kin + near)
    ]

    def find(group):
        keys_own = own_key + 3 * group

        def one(rel, carry):
            owner_u = u + (rel % 2) * (SIDE - 1 - 2 * u)
            owner = at(owner_u, ring(rel // 2))
            for third in range(3):
                for p in range(rows):
                    base = p * slots_row
                    if third:
                        t = 3 if third == 1 else 2
                        base = meta[keys_own, pattern_at + p * pattern + t] * slots_row
                    for c in range(vel_rows):
                        wanted = owner * vel_rows + c
                        first, second = jnp.int32(-1), jnp.int32(-1)
                        for l in range(slots_row):
                            hit = meta[keys_own + third, base + l] == wanted
                            second = jnp.where(hit, first, second)
                            first = jnp.where(hit, max(third - 1, 0) * listed + base + l, first)
                        entry = ((third * rows + p) * vel_rows + c) * 2
                        picks[group * CLASS + rel, entry] = first
                        picks[group * CLASS + rel, entry + 1] = second
            return carry

        lax.fori_loop(0, CLASS, one, 0)

    def spread(group, thirds):
        home, beside = ((div_own, div_own_side), (div_mate, div_mate_side))[group]

        def one(rel, carry):
            place = group * CLASS + rel
            for third in thirds:
                source = beside if third else home
                for p in range(rows):
                    for c in range(vel_rows):
                        entry = ((third * rows + p) * vel_rows + c) * 2
                        first, second = picks[place, entry], picks[place, entry + 1]
                        one_on = jnp.where(first >= 0, 1.0, 0.0)
                        two_on = jnp.where(second >= 0, 1.0, 0.0)
                        value = (
                            one_on * source[jnp.maximum(first, 0)]
                            + two_on * source[jnp.maximum(second, 0)]
                        )
                        high, low = halves(value)
                        lines = slice(p * side, (p + 1) * side)
                        at_high = slice(c * side, (c + 1) * side)
                        at_low = slice(width + c * side, width + (c + 1) * side)
                        dense_div[place, third, lines, at_high] = high
                        dense_div[place, third, lines, at_low] = low
            return carry

        lax.fori_loop(0, CLASS, one, 0)

    def gather(rel):
        for v in range(vel_rows):
            for column in range(columns):
                place = meta[rel, inv_at + v * columns + column]
                on = jnp.where(place >= 0, 1.0, 0.0)
                high, low = halves(on * held[rel][v * inv_slots + jnp.maximum(place, 0)])
                third = (1, 0, 2)[column // vel_rows]
                c = column % vel_rows
                lines = slice(v * side, (v + 1) * side)
                dense_inv[rel, third, lines, c * side : (c + 1) * side] = high
                dense_inv[rel, third, lines, width + c * side : width + (c + 1) * side] = low

    def product(rel, group, only=None):
        place = group * CLASS + rel
        factors = []
        for third in range(3):
            inv = dense_inv[rel, third]
            div = dense_div[place, third]
            inv_high, inv_low = inv[:, :width], inv[:, width:]
            div_high, div_low = div[:, :width], div[:, width:]
            value = lax.dot_general(
                jnp.concatenate([inv_high, inv_high, inv_low], axis=1),
                jnp.concatenate([div_high, div_low, div_high], axis=1),
                (((1,), (1,)), ((), ())),
                preferred_element_type=F32,
            )
            factors.append(halves(value))
        for p in range(rows):
            order = ((0, p), (0, 1 - p), (2, p), (1, p))
            high, low = (
                jnp.concatenate(
                    [factors[third][i][:, q * side : (q + 1) * side] for third, q in order], axis=1
                )
                for i in range(2)
            )
            left = dense_div[place, 0, p * side : (p + 1) * side, :]
            left_high, left_low = left[:, :width], left[:, width:]
            sums[group, p] += jnp.dot(
                jnp.concatenate([left_high, left_high, left_low], axis=1),
                jnp.concatenate([high, low, high], axis=0),
                preferred_element_type=F32,
            )
            if only is not None:
                only[p].start()

    for copy in meta_copies:
        copy.start()
    cross_first.start()
    ring_last[0].start()
    ring_last[1].start()
    ring_own[0].start()
    ring_own[1].start()
    cross_last[0].start()
    div_copies[0].start()
    div_copies[1].start()
    div_copies[2].start()
    div_copies[3].start()
    div_copies[4].start()
    sums[...] = jnp.zeros_like(sums)
    own_inv.wait()
    own_div.wait()
    cross_first.wait_recv()
    ring_far[0].start()
    ring_far[1].start()
    ring_last[0].wait_recv()
    ring_last[3].start()
    cross_last[2].start()
    ring_last[1].wait_recv()
    ring_last[2].start()
    cross_last[1].start()
    for copy in meta_copies:
        copy.wait_recv()
    find(0)
    div_copies[0].wait_recv()
    div_copies[5].start()
    div_copies[6].start()
    ring_own[0].wait_recv()
    ring_own[3].start()
    ring_own[1].wait_recv()
    ring_own[2].start()
    div_copies[1].wait_recv()
    div_copies[7].start()
    div_copies[8].start()
    find(1)
    spread(0, (0,))
    ring_last[2].wait_recv()
    cross_last[3].start()
    ring_last[3].wait_recv()
    cross_last[4].start()
    div_copies[2].wait_recv()
    div_copies[3].wait_recv()
    spread(0, (1,2,))
    gather(0)
    product(0, 0)
    ring_far[0].wait_recv()
    ring_far[3].start()
    ring_far[1].wait_recv()
    ring_far[2].start()
    cross_last[0].wait_recv()
    gather(1)
    product(1, 0)
    gather(2)
    product(2, 0)
    gather(6)
    product(6, 0)
    div_copies[4].wait_recv()
    spread(1, (0,))
    ring_own[2].wait_recv()
    ring_own[3].wait_recv()
    gather(4)
    product(4, 0)
    cross_last[2].wait_recv()
    gather(3)
    cross_last[1].wait_recv()
    gather(7)
    div_copies[5].wait_recv()
    div_copies[6].wait_recv()
    div_copies[7].wait_recv()
    div_copies[8].wait_recv()
    spread(1, (1,2,))
    product(0, 1)
    product(1, 1)
    product(2, 1)
    product(6, 1)
    product(4, 1)
    product(3, 1)
    product(7, 1)
    cross_last[3].wait_recv()
    cross_last[4].wait_recv()
    ring_far[2].wait_recv()
    ring_far[3].wait_recv()
    gather(5)
    returns = [
        remote(
            sums.at[1, pl.ds(p, 1)],
            given.at[pl.ds(p, 1)],
            sum_send.at[p],
            sum_recv.at[p],
            (mate_row, col),
        )
        for p in range(rows)
    ]
    product(5, 1, returns)
    product(3, 0)
    product(7, 0)
    product(5, 0)
    for p in range(rows):
        returns[p].wait_recv()
        total = sums[0, p] + given[p]
        for t in range(pattern):
            kept = jnp.where(t < pattern_count_ref[p], 1.0, 0.0)
            out_ref[p, t] = kept * total[:, t * side : (t + 1) * side]

    for copy in (*meta_copies, *div_copies, *made, *returns):
        copy.wait_send()


def local(
    lon_count,
    div_blocks,
    div_owner,
    div_local,
    div_count,
    inv_blocks,
    inv_cols,
    inv_count,
    schur_cols,
    schur_count,
):
    rows, slots_row, side, _ = div_blocks.shape
    vel_rows, inv_slots = inv_cols.shape
    pattern = schur_cols.shape[1]
    listed = rows * slots_row
    width = pattern * side
    ints = (div_owner, div_local, div_count, inv_cols, inv_count, schur_cols, schur_count)
    operands = [
        pltpu.with_memory_space_constraint(value, pltpu.HBM)
        for value in (
            *ints,
            div_blocks.reshape(listed, side, side),
            inv_blocks.reshape(vel_rows * inv_slots, side, side),
        )
    ]
    return pl.pallas_call(
        functools.partial(kernel, lon_count),
        out_shape=jax.ShapeDtypeStruct((rows, pattern, side, side), F32),
        in_specs=[pl.BlockSpec(memory_space=pltpu.HBM)] * len(operands),
        out_specs=pl.BlockSpec(memory_space=pltpu.VMEM),
        scratch_shapes=[
            *[pltpu.VMEM((vel_rows * inv_slots, side, side), F32)] * CLASS,
            pltpu.VMEM((listed, side, side), F32),
            pltpu.VMEM((2 * listed, side, side), F32),
            pltpu.VMEM((listed, side, side), F32),
            pltpu.VMEM((2 * listed, side, side), F32),
            pltpu.VMEM((listed, side, side), F32),
            pltpu.VMEM((2 * CLASS, 3, rows * side, 2 * vel_rows * side), BF16),
            pltpu.VMEM((CLASS, 3, vel_rows * side, 2 * vel_rows * side), BF16),
            pltpu.VMEM((2, rows, side, width), F32),
            pltpu.VMEM((rows, side, width), F32),
            pltpu.SMEM((1, META_WIDTH), jnp.int32),
            pltpu.SMEM((CLASS + 6, META_WIDTH), jnp.int32),
            pltpu.SMEM((2 * CLASS, 6 * rows * vel_rows), jnp.int32),
            *[pltpu.SMEM(value.shape, jnp.int32) for value in ints],
            pltpu.SemaphoreType.DMA((9,)),
            pltpu.SemaphoreType.DMA((9,)),
            pltpu.SemaphoreType.DMA((9,)),
            pltpu.SemaphoreType.DMA((12,)),
            pltpu.SemaphoreType.DMA((12,)),
            pltpu.SemaphoreType.DMA((18,)),
            pltpu.SemaphoreType.DMA((18,)),
            pltpu.SemaphoreType.DMA((rows,)),
            pltpu.SemaphoreType.DMA((rows,)),
        ],
        compiler_params=pltpu.CompilerParams(
            collective_id=0, has_side_effects=True, vmem_limit_bytes=56 * 2**20
        ),
    )(*operands)


def solution(mesh):
    placed = (
        P(("row", "col"), None, None, None),
        P(("row", "col"), None),
        P(("row", "col"), None),
        P(("row", "col")),
        P(("row", "col"), None, None, None),
        P(("row", "col"), None),
        P(("row", "col")),
        P(("row", "col"), None),
        P(("row", "col")),
    )
    return jax.shard_map(
        functools.partial(local, mesh.shape["col"]),
        mesh=mesh,
        in_specs=placed,
        out_specs=P(("row", "col"), None, None, None),
        check_vma=False,
    )
```
